32 devices in a mesh: parts: 2 (over x), seq: 16 (over z, y, core).
Axes of the slice: x: 2, y: 2, z: 4, core: 2. Of those that a mesh axis runs over, the one named last changes fastest.
Arguments:
- queries: bfloat16 [2, 4, 8192], P(None, 'parts'), parts along dimension 1, may hold values from -7 to 7
- cache_k: bfloat16 [65536, 1024], P(('parts', 'seq')), parts along dimension 0, may hold values from -15 to 15
- cache_v: bfloat16 [65536, 1024], P(('parts', 'seq')), parts along dimension 0, may hold values from -6 to 6
- context_len: int32 [4], P('parts'), parts along dimension 0, may hold values from 8192 to 16384, as said below
- slot_seq: int32 [65536], P(('parts', 'seq')), parts along dimension 0, may hold values from 0 to 2, as said below
- slot_pos: int32 [65536], P(('parts', 'seq')), parts along dimension 0, may hold values from 0 to 16383, as said below
Outputs:
- attended: bfloat16 [2, 4, 8192], P(None, 'parts'), parts along dimension 1
The draws below stay inside these ranges and needn't reach their ends.
There are 2 independent parts, one for each index of `parts`. The reference program is written for one: setup_inputs(seed, part) draws one part's arguments, and reference() takes and returns one part's arrays. A program takes and returns all parts, laid end to end along the dimension named above; each array names one. Nothing has to cross between parts.
Inputs may be any that keep to these rules, and one draw needn't show every extreme that they name: Each sequence s has exactly context_len[s] slots with slot_seq = s; some sequence has exactly 16384. `slot_seq`: aligned blocks of 128 slots belong to one sequence or are free; the slots of a sequence hold each position from 0 to context_len[s] - 1 exactly once; free slots carry 2. `slot_pos`: 0 on free slots.
All inputs are finite; a program needn't handle non-finite values.
Results may differ from the reference program's by a relative error of at most 0.006.
Values may be sent and summed in bfloat16 or wider, within the bound.
A program may use at most 64 MiB of HBM per device.

```python
import jax
import jax.numpy as jnp
from jax import lax

QH = 64
KVH = 8
HD = 128
GROUP = 8
SEQS = 2
SLOT_DEV = 2048
BLOCK = 128
SLOTS = 32768
LEN_MAX = 16384
LEN_MIN = 8192
N_SEQ = 16


def cache_layout(key):
    base = jax.random.fold_in(key, 7)
    first_key, second_key, third_key = jax.random.split(base, 3)
    drawn = jax.random.randint(first_key, (SEQS,), LEN_MIN, LEN_MAX + 1).astype(jnp.int32)
    longest = jax.random.randint(third_key, (), 0, SEQS).astype(jnp.int32)
    seq_range = jnp.arange(SEQS, dtype=jnp.int32)
    lengths = jnp.where(seq_range == longest, jnp.int32(LEN_MAX), drawn).astype(jnp.int32)
    needed = (lengths + BLOCK - 1) // BLOCK
    block_ends = jnp.cumsum(needed)
    block_starts = block_ends - needed
    block_count = SLOTS // BLOCK
    shuffle = jax.random.permutation(second_key, block_count).astype(jnp.int32)
    rank_ids = jnp.arange(block_count, dtype=jnp.int32)
    owners = jnp.sum((rank_ids[:, None] >= block_ends[None, :]).astype(jnp.int32), axis=1)
    clipped = jnp.minimum(owners, SEQS - 1)
    within = rank_ids - block_starts[clipped]
    owner_phys = jnp.zeros((block_count,), jnp.int32).at[shuffle].set(owners)
    within_phys = jnp.zeros((block_count,), jnp.int32).at[shuffle].set(within)
    slot_ids = jnp.arange(SLOTS, dtype=jnp.int32)
    block_ids = slot_ids // BLOCK
    seq_of = owner_phys[block_ids]
    pos_of = within_phys[block_ids] * BLOCK + slot_ids % BLOCK
    length_of = lengths[jnp.minimum(seq_of, SEQS - 1)]
    valid = (seq_of < SEQS) & (pos_of < length_of)
    seq_of = jnp.where(valid, seq_of, SEQS).astype(jnp.int32)
    pos_of = jnp.where(valid, pos_of, 0).astype(jnp.int32)
    return (lengths, seq_of, pos_of)


def draw_context_len(key, part):
    return cache_layout(key)[0]


def draw_slot_seq(key, part):
    return cache_layout(key)[1]


def draw_slot_pos(key, part):
    return cache_layout(key)[2]


def draw_cache_k(key, part):
    own_key = jax.random.fold_in(key, 23)
    keys_out = jnp.clip(2.5 * jax.random.normal(own_key, (SLOTS, KVH * HD), jnp.float32), -15.0, 15.0)
    return keys_out.astype(jnp.bfloat16)


def draw_queries(key, part):
    own_key = jax.random.fold_in(key, 31)
    query_out = jnp.clip(jax.random.normal(own_key, (2, SEQS, QH, HD), jnp.float32), -6.0, 6.0)
    return query_out.reshape(2, SEQS, QH * HD).astype(jnp.bfloat16)


def level_of(stream_key, shape, shards, smallest, high):
    def one(position, shards_of):
        draws = jax.random.uniform(jax.random.fold_in(jax.random.fold_in(stream_key, 6), position), (shards_of,), jnp.float32, smallest / len(shards), high / len(shards))
        return jnp.repeat(jnp.exp(draws), shape[position] // shards_of).reshape((-1,) + (1,) * (len(shape) - position - 1))

    factor_of = one(*shards[0])
    for cut in shards[1:]:
        factor_of = factor_of * one(*cut)
    return factor_of


def scatter_about(rng, dims, deviation, limit, cuts=(), kind=jnp.bfloat16):
    entries = jax.random.normal(rng, dims, jnp.float32) * deviation
    if len(cuts) > 0:
        entries = level_of(rng, dims, cuts, -0.22, 0.18) * entries
    return jnp.clip(entries, min=-limit, max=limit).astype(kind)


def setup_inputs(seed: int = 0, part: int = 0) -> dict:
    seeds = jax.random.split(jax.random.key(seed), 7)
    part_splits = jax.random.split(jax.random.fold_in(seeds[6], part), 7)
    return {
        "queries": draw_queries(jax.random.fold_in(jax.random.fold_in(seeds[6], part), 71), part),
        "cache_k": draw_cache_k(jax.random.fold_in(jax.random.fold_in(seeds[6], part), 71), part),
        "cache_v": scatter_about(part_splits[2], (SLOTS, KVH * HD), 1.0, 6.0, ((0, 16),)),
        "context_len": draw_context_len(jax.random.fold_in(jax.random.fold_in(seeds[6], part), 71), part),
        "slot_seq": draw_slot_seq(jax.random.fold_in(jax.random.fold_in(seeds[6], part), 71), part),
        "slot_pos": draw_slot_pos(jax.random.fold_in(jax.random.fold_in(seeds[6], part), 71), part),
    }


def visible_slots(seq_block, pos_block, context_len):
    seq_ids = jnp.arange(SEQS, dtype=jnp.int32)
    step_ids = jnp.arange(2, dtype=jnp.int32)
    owners = seq_block[None, :] == seq_ids[:, None]
    last_visible = context_len[None, :] - 2 + step_ids[:, None]
    allowed = owners[None, :, :] & (pos_block[None, None, :] <= last_visible[:, :, None])
    return allowed[:, :, None, None, :]


def block_scores(query_heads, key_block):
    key_rows = key_block.astype(jnp.float32).reshape(SLOT_DEV, KVH, HD)
    scores = jnp.einsum('tsghd,ngd->tsghn', query_heads, key_rows, precision=lax.Precision.HIGHEST)
    return scores * (HD ** -0.5)


def reference(queries, cache_k, cache_v, context_len, slot_seq, slot_pos):
    query_heads = queries.astype(jnp.float32).reshape(2, SEQS, KVH, GROUP, HD)
    key_blocks = cache_k.reshape(N_SEQ, SLOT_DEV, KVH * HD)
    value_blocks = cache_v.reshape(N_SEQ, SLOT_DEV, KVH * HD)
    seq_blocks = slot_seq.reshape(N_SEQ, SLOT_DEV)
    pos_blocks = slot_pos.reshape(N_SEQ, SLOT_DEV)

    def block_max(inputs):
        key_block, seq_block, pos_block = inputs
        scores = block_scores(query_heads, key_block)
        allowed = visible_slots(seq_block, pos_block, context_len)
        return jnp.max(jnp.where(allowed, scores, jnp.float32(-1e30)), axis=-1)

    highest = jnp.max(lax.map(block_max, (key_blocks, seq_blocks, pos_blocks)), axis=0)

    def accumulate(carry, inputs):
        denom, numer = carry
        key_block, value_block, seq_block, pos_block = inputs
        scores = block_scores(query_heads, key_block)
        allowed = visible_slots(seq_block, pos_block, context_len)
        weights = jnp.where(allowed, jnp.exp(scores - highest[..., None]), jnp.float32(0.0))
        denom = denom + jnp.sum(weights, axis=-1)
        rounded = lax.optimization_barrier(weights.astype(jnp.bfloat16)).astype(jnp.float32)
        value_rows = value_block.astype(jnp.float32).reshape(SLOT_DEV, KVH, HD)
        numer = numer + jnp.einsum('tsghn,ngd->tsghd', rounded, value_rows, precision=lax.Precision.HIGHEST)
        return (denom, numer), None

    start = (jnp.zeros((2, SEQS, KVH, GROUP), jnp.float32), jnp.zeros((2, SEQS, KVH, GROUP, HD), jnp.float32))
    (denom, numer), _ = lax.scan(accumulate, start, (key_blocks, value_blocks, seq_blocks, pos_blocks))
    attended = (numer / denom[..., None]).astype(jnp.bfloat16)
    return attended.reshape(2, SEQS, QH * HD)
```

```python
import functools

import jax
import jax.numpy as jnp
from jax import lax
from jax.experimental import pallas as pl
from jax.experimental.pallas import tpu as pltpu
from jax.sharding import PartitionSpec as P

KVH = 8
HD = 128
CHUNKS = 4
PER_CORE = CHUNKS // 2
LIMIT = 20 << 20
SHIFT = HD ** (-0.5) * 1.4426950408889634
HIDDEN = -1e30
MESH = pl.DeviceIdType.MESH


def served_by(plane, planes):
    return (planes // 2) * ((4 * plane // planes + 2) // 3)


def root_planes(planes):
    return (0, planes // 2) if planes > 1 else (0,)


def kernel(
    n, ctx_hbm, q_hbm, k_hbm, v_hbm, seq_hbm, pos_hbm, out,
    ctx, q_ref, seq_ref, pos_ref, kbuf, vbuf, qf, bias,
    half_num, half_ml, peer_num, peer_ml, chip_num, chip_ml,
    isem, ksem, vsem, hs, hsm, hr, hrm, cs, csm, cr, crm, ps, pr, fs, fr,
):
    me = lax.axis_index("seq")
    chips = n // 2
    planes = chips // 2
    core = me % 2
    chip = me // 2
    y = chip % 2
    plane = chip // 2
    roots = root_planes(planes)
    is_root = functools.reduce(lambda a, b: a | b, [plane == r for r in roots])
    partner = chip * 2 + (1 - core)
    server = served_by(plane, planes) * 2 + y
    guests = {r: [p for p in range(planes) if p not in roots and served_by(p, planes) == r] for r in roots}
    heads_each = KVH // CHUNKS
    width = heads_each * HD
    group = q_ref.shape[2] // HD // KVH
    seqs = q_ref.shape[1]
    rows = 2 * seqs * group
    block = heads_each * rows
    tile = group * seqs
    span = heads_each * tile

    barrier = pltpu.get_barrier_semaphore()

    def greet(device):
        pl.semaphore_signal(barrier, inc=1, device_id={"seq": device}, device_id_type=MESH)

    inputs = []
    for i, (src, dst) in enumerate(((q_hbm, q_ref), (seq_hbm, seq_ref), (pos_hbm, pos_ref), (ctx_hbm, ctx))):
        copy = pltpu.make_async_copy(src, dst, isem.at[i])
        copy.start()
        inputs.append(copy)

    def kv(i):
        first = pl.multiple_of(((1 - core) * PER_CORE + i) % CHUNKS * width, width)
        columns = pl.ds(first, width)
        return (
            lambda: pltpu.make_async_copy(k_hbm.at[:, columns], kbuf.at[i], ksem.at[i]),
            lambda: pltpu.make_async_copy(v_hbm.at[:, columns], vbuf.at[i], vsem.at[i]),
        )

    def load(i, carry):
        for copy in kv(i):
            copy().start()
        return carry

    lax.fori_loop(0, CHUNKS, load, 0)

    greet(partner)

    @pl.when(is_root)
    def _():
        for k in range(1, chips):
            greet((chip + k) % chips * 2 + core)

    @pl.when(jnp.logical_not(is_root))
    def _():
        for d in range(2):
            greet(server * 2 + d)

    for copy in inputs:
        copy.wait()

    for t in range(2):
        for head in range(KVH * group):
            g, h = head // group, head % group
            base = g * rows + t * group * seqs + h * seqs
            qf[base : base + seqs, :] = q_ref[t, :, head * HD : (head + 1) * HD].astype(jnp.float32)

    slots = k_hbm.shape[0]
    row_ids = lax.broadcasted_iota(jnp.int32, (rows, 128), 0)
    row_seq = row_ids % seqs
    row_step = row_ids // (group * seqs)
    last = jnp.zeros((rows, 128), jnp.int32)
    for s in range(seqs):
        last = jnp.where(row_seq == s, ctx[s], last)
    last = last - 2 + row_step
    for b in range(slots // 128):
        cut = slice(b * 128, (b + 1) * 128)
        owner = jnp.broadcast_to(seq_ref[:, cut], (rows, 128))
        pos = jnp.broadcast_to(pos_ref[:, cut], (rows, 128))
        allowed = (owner == row_seq) & (pos <= last)
        bias[:, cut] = jnp.where(allowed, 0.0, HIDDEN)

    lane = lax.broadcasted_iota(jnp.int32, (rows, 128), 1)

    def score(i):
        kv(i)[0]().wait()
        probs = []
        packed = []
        for e in range(heads_each):
            head = ((1 - core) * PER_CORE + i) % CHUNKS * heads_each + e
            q = qf[pl.ds(pl.multiple_of(head * rows, rows), rows), :].astype(jnp.bfloat16)
            scores = lax.dot_general(
                q, kbuf[i, :, e * HD : (e + 1) * HD], (((1,), (1,)), ((), ())),
                preferred_element_type=jnp.float32,
            ) + bias[...]
            m = jnp.max(scores, axis=-1, keepdims=True)
            w = jnp.exp2((scores - m) * SHIFT)
            l = jnp.sum(w, axis=-1, keepdims=True)
            probs.append(w.astype(jnp.bfloat16))
            packed.append(jnp.where(lane == 0, m, l))
        packed = packed + [jnp.zeros((128 - block, 128), jnp.float32)]
        return probs, jnp.transpose(jnp.concatenate(packed, axis=0))[:2, :]

    def gather(i, probs):
        kv(i)[1]().wait()
        return jnp.concatenate(
            [
                jnp.dot(probs[e], vbuf[i, :, e * HD : (e + 1) * HD], preferred_element_type=jnp.float32)
                for e in range(heads_each)
            ],
            axis=0,
        )

    def remote(src, dst, ss, rs, device):
        return pltpu.make_async_remote_copy(
            src_ref=src, dst_ref=dst, send_sem=ss, recv_sem=rs, device_id={"seq": device}, device_id_type=MESH
        )

    def to_partner(j):
        return (
            remote(half_ml.at[j], peer_ml.at[j], hsm.at[j], hrm.at[j], partner),
            remote(half_num.at[j], peer_num.at[j], hs.at[j], hr.at[j], partner),
        )

    targets = [r * 2 + side for r in roots for side in range(2)]

    def to_root(j, i):
        device = targets[i] * 2 + core
        return (
            remote(chip_ml.at[j, chip], chip_ml.at[j, chip], csm.at[j, i], crm.at[j, chip], device),
            remote(chip_num.at[j, chip], chip_num.at[j, chip], cs.at[j, i], cr.at[j, chip], device),
        )

    def from_chip(j, k):
        slot = (chip + k) % chips
        return (
            remote(chip_ml.at[j, slot], chip_ml.at[j, slot], csm.at[j, 0], crm.at[j, slot], slot * 2 + core),
            remote(chip_num.at[j, slot], chip_num.at[j, slot], cs.at[j, 0], cr.at[j, slot], slot * 2 + core),
        )

    def part(owner, j):
        return out.at[:, pl.ds(pl.multiple_of(owner * (PER_CORE * span) + j * span, span), span), :]

    for j in range(PER_CORE):
        probs, ml = score(j)
        half_ml[j] = ml
        half_num[j] = gather(j, probs).astype(jnp.bfloat16)
        if j == 0:
            for r in roots:
                @pl.when(plane == r)
                def _():
                    pl.semaphore_wait(barrier, len(targets) + 2 * len(guests[r]))

            @pl.when(jnp.logical_not(is_root))
            def _():
                pl.semaphore_wait(barrier, 1 + len(targets))
        for copy in to_partner(j):
            copy.start()

    for j in range(PER_CORE):
        probs, ml = score(PER_CORE + j)
        numer = gather(PER_CORE + j, probs)
        for copy in to_partner(j):
            copy.wait_recv()
        other = peer_ml[j]
        top = jnp.maximum(ml[0:1], other[0:1])
        mine = jnp.exp2((ml[0:1] - top) * SHIFT)
        theirs = jnp.exp2((other[0:1] - top) * SHIFT)
        chip_ml[j, chip] = jnp.concatenate([top, mine * ml[1:2] + theirs * other[1:2]], axis=0)
        columns = jnp.transpose(jnp.concatenate([mine, theirs, jnp.zeros((6, 128), jnp.float32)], axis=0))
        total = numer * columns[:block, 0:1] + peer_num[j].astype(jnp.float32) * columns[:block, 1:2]
        chip_num[j, chip] = total.astype(jnp.bfloat16)
        for i, target in enumerate(targets):
            @pl.when(chip != target)
            def _():
                for copy in to_root(j, i):
                    copy.start()

    @pl.when(is_root)
    def _():
        for j in range(PER_CORE):
            for k in range(1, chips):
                for copy in from_chip(j, k):
                    copy.wait_recv()
            maxima = [chip_ml[j, i][0:1] for i in range(chips)]
            top = functools.reduce(jnp.maximum, maxima)
            factors = [jnp.exp2((m - top) * SHIFT) for m in maxima]
            denom = sum(f * chip_ml[j, i][1:2] for i, f in enumerate(factors))
            factors = [f / denom for f in factors]
            pad = -chips % 8
            if pad:
                factors = factors + [jnp.zeros((pad, 128), jnp.float32)]
            columns = jnp.transpose(jnp.concatenate(factors, axis=0))
            numer = None
            for i in range(chips):
                term = chip_num[j, i].astype(jnp.float32) * columns[:block, i : i + 1]
                numer = term if numer is None else numer + term
            attended = numer.astype(jnp.bfloat16)
            for e in range(heads_each):
                for t in range(2):
                    base = pl.multiple_of(core * (PER_CORE * span) + j * span + e * tile, tile)
                    out[t, pl.ds(base, tile), :] = attended[e * rows + t * tile : e * rows + (t + 1) * tile]
            remote(part(core, j), part(core, j), ps.at[j], pr.at[j], partner).start()
            for r in roots:
                if guests[r]:
                    @pl.when(plane == r)
                    def _():
                        for i, guest in enumerate(guests[r]):
                            for d in range(2):
                                device = (guest * 2 + y) * 2 + d
                                remote(part(core, j), part(core, j), fs.at[j, i, d], fr.at[j, core], device).start()
        for j in range(PER_CORE):
            remote(part(core, j), part(1 - core, j), ps.at[j], pr.at[j], partner).wait_recv()
        for j in range(PER_CORE):
            remote(part(core, j), part(core, j), ps.at[j], pr.at[j], partner).wait_send()
            for r in roots:
                if guests[r]:
                    @pl.when(plane == r)
                    def _():
                        for i, guest in enumerate(guests[r]):
                            for d in range(2):
                                device = (guest * 2 + y) * 2 + d
                                remote(part(core, j), part(core, j), fs.at[j, i, d], fr.at[j, core], device).wait_send()

    @pl.when(jnp.logical_not(is_root))
    def _():
        for j in range(PER_CORE):
            for d in range(2):
                remote(part(d, j), part(d, j), fs.at[j, 0, d], fr.at[j, d], server * 2 + d).wait_recv()

    for j in range(PER_CORE):
        for copy in to_partner(j):
            copy.wait_send()
        for i, target in enumerate(targets):
            @pl.when(chip != target)
            def _():
                for copy in to_root(j, i):
                    copy.wait_send()


def per_device(n, queries, cache_k, cache_v, context_len, slot_seq, slot_pos):
    slots = cache_k.shape[0]
    seqs = queries.shape[1]
    heads = queries.shape[2] // HD
    rows = 2 * seqs * heads // KVH
    heads_each = KVH // CHUNKS
    block = heads_each * rows
    chips = n // 2
    fans = 2 * len(root_planes(chips // 2))
    vmem = pl.BlockSpec(memory_space=pltpu.VMEM)
    dma = pltpu.SemaphoreType.DMA
    anywhere = pl.BlockSpec(memory_space=pltpu.HBM)
    attended = pl.pallas_call(
        functools.partial(kernel, n),
        out_shape=jax.ShapeDtypeStruct((2, heads * seqs, HD), jnp.bfloat16),
        in_specs=[anywhere] * 6,
        out_specs=vmem,
        scratch_shapes=[
            pltpu.SMEM((seqs,), jnp.int32),
            pltpu.VMEM(queries.shape, jnp.bfloat16),
            pltpu.VMEM((1, slots), jnp.int32),
            pltpu.VMEM((1, slots), jnp.int32),
            pltpu.VMEM((CHUNKS, slots, heads_each * HD), jnp.bfloat16),
            pltpu.VMEM((CHUNKS, slots, heads_each * HD), jnp.bfloat16),
            pltpu.VMEM((KVH * rows, HD), jnp.float32),
            pltpu.VMEM((rows, slots), jnp.float32),
            pltpu.VMEM((PER_CORE, block, HD), jnp.bfloat16),
            pltpu.VMEM((PER_CORE, 2, 128), jnp.float32),
            pltpu.VMEM((PER_CORE, block, HD), jnp.bfloat16),
            pltpu.VMEM((PER_CORE, 2, 128), jnp.float32),
            pltpu.VMEM((PER_CORE, chips, block, HD), jnp.bfloat16),
            pltpu.VMEM((PER_CORE, chips, 2, 128), jnp.float32),
            dma((4,)), dma((CHUNKS,)), dma((CHUNKS,)),
            dma((PER_CORE,)), dma((PER_CORE,)), dma((PER_CORE,)), dma((PER_CORE,)),
            dma((PER_CORE, fans)), dma((PER_CORE, fans)), dma((PER_CORE, chips)), dma((PER_CORE, chips)),
            dma((PER_CORE,)), dma((PER_CORE,)),
            dma((PER_CORE, chips // 2, 2)), dma((PER_CORE, 2)),
        ],
        compiler_params=pltpu.CompilerParams(collective_id=0, has_side_effects=True, vmem_limit_bytes=LIMIT),
    )(*[
        pltpu.with_memory_space_constraint(x, pltpu.HBM)
        for x in (context_len, queries, cache_k, cache_v, slot_seq.reshape(1, slots), slot_pos.reshape(1, slots))
    ])
    steps = queries.shape[0]
    return attended.reshape(steps, heads, seqs, HD).transpose(0, 2, 1, 3).reshape(queries.shape)


def solution(mesh):
    return jax.shard_map(
        functools.partial(per_device, mesh.shape["seq"]),
        mesh=mesh,
        in_specs=(
            P(None, "parts", None),
            P(("parts", "seq"), None),
            P(("parts", "seq"), None),
            P("parts"),
            P(("parts", "seq")),
            P(("parts", "seq")),
        ),
        out_specs=P(None, "parts", None),
        check_vma=False,
    )
```

```python
import functools

import jax
import jax.numpy as jnp
from jax import lax
from jax.experimental import pallas as pl
from jax.experimental.pallas import tpu as pltpu
from jax.sharding import PartitionSpec as P

KVH = 8
HD = 128
CHUNKS = 2
STEP = 256
LIMIT = 24 << 20
SHIFT = HD ** (-0.5) * 1.4426950408889634
HIDDEN = -1e30
MESH = pl.DeviceIdType.MESH


def served_by(plane, planes):
    return (planes // 2) * ((4 * plane // planes + 2) // 3)


def root_planes(planes):
    return (0, planes // 2) if planes > 1 else (0,)


def kernel(
    n, ctx_hbm, q_hbm, k_hbm, v_hbm, seq_hbm, pos_hbm, out,
    ctx, q_ref, seq_ref, pos_ref, kbuf, vbuf, qf, qt, bias, sbuf, pbuf,
    half_num, half_ml, peer_num, peer_ml, chip_num, chip_ml,
    isem, ksem, vsem, hs, hsm, hr, hrm, cs, csm, cr, crm, ps, pr, fs, fr,
):
    me = lax.axis_index("seq")
    chips = n // 2
    planes = chips // 2
    core = me % 2
    chip = me // 2
    y = chip % 2
    plane = chip // 2
    roots = root_planes(planes)
    is_root = functools.reduce(lambda a, b: a | b, [plane == r for r in roots])
    partner = chip * 2 + (1 - core)
    server = served_by(plane, planes) * 2 + y
    guests = {r: [p for p in range(planes) if p not in roots and served_by(p, planes) == r] for r in roots}
    halves = (1 - core, core)
    slots = k_hbm.shape[0]
    heads_half = KVH // 2
    heads_each = heads_half // CHUNKS
    wide = heads_half * HD
    width = heads_each * HD
    group = q_ref.shape[2] // HD // KVH
    seqs = q_ref.shape[1]
    rows = 2 * seqs * group
    lanes = heads_half * rows
    block = heads_each * rows
    tile = group * seqs
    span = heads_each * tile
    cut = slots // CHUNKS

    barrier = pltpu.get_barrier_semaphore()

    def greet(device):
        pl.semaphore_signal(barrier, inc=1, device_id={"seq": device}, device_id_type=MESH)

    inputs = []
    for i, (src, dst) in enumerate(((q_hbm, q_ref), (seq_hbm, seq_ref), (pos_hbm, pos_ref), (ctx_hbm, ctx))):
        copy = pltpu.make_async_copy(src, dst, isem.at[i])
        copy.start()
        inputs.append(copy)

    def first_column(order):
        half = core * order + (1 - core) * (1 - order)
        return half * wide

    def k_copy(i):
        order, part = i // CHUNKS, i % CHUNKS
        some = pl.ds(pl.multiple_of(part * cut, cut), cut)
        columns = pl.ds(pl.multiple_of(first_column(order), wide), wide)
        return pltpu.make_async_copy(k_hbm.at[some, columns], kbuf.at[order, some], ksem.at[i])

    def v_copy(i):
        order, part = i // CHUNKS, i % CHUNKS
        columns = pl.ds(pl.multiple_of(first_column(order) + part * width, width), width)
        return pltpu.make_async_copy(v_hbm.at[:, columns], vbuf.at[i], vsem.at[i])

    def load_k(i, carry):
        k_copy(i).start()
        return carry

    def load_v(i, carry):
        v_copy(i).start()
        return carry

    lax.fori_loop(0, 2 * CHUNKS, load_k, 0)
    lax.fori_loop(0, 2 * CHUNKS, load_v, 0)

    greet(partner)

    @pl.when(is_root)
    def _():
        for k in range(1, chips):
            greet((chip + k) % chips * 2 + core)

    @pl.when(jnp.logical_not(is_root))
    def _():
        for d in range(2):
            greet(server * 2 + d)

    for copy in inputs:
        copy.wait()

    for t in range(2):
        for head in range(KVH * group):
            g, h = head // group, head % group
            base = g * rows + t * group * seqs + h * seqs
            qf[base : base + seqs, :] = q_ref[t, :, head * HD : (head + 1) * HD].astype(jnp.float32)

    column = lax.broadcasted_iota(jnp.int32, (HD, lanes), 1)
    for order in range(2):
        turned = jnp.transpose(qf[pl.ds(pl.multiple_of(halves[order] * lanes, lanes), lanes), :])
        for e in range(heads_half):
            qt[order, e * HD : (e + 1) * HD, :] = jnp.where(column // rows == e, turned, 0.0).astype(jnp.bfloat16)

    masks = []
    for t in range(2):
        for sq in range(seqs):
            allowed = (seq_ref[...] == sq) & (pos_ref[...] <= ctx[sq] - 2 + t)
            masks.append(jnp.where(allowed, 0.0, HIDDEN))
    pad = -len(masks) % 16
    masks = jnp.concatenate(masks + [jnp.zeros((pad, slots), jnp.float32)], axis=0).astype(jnp.bfloat16)
    pick_row = lax.broadcasted_iota(jnp.int32, (2 * seqs + pad, lanes), 0)
    pick_lane = lax.broadcasted_iota(jnp.int32, (2 * seqs + pad, lanes), 1) % rows
    pick = (pick_lane // tile) * seqs + pick_lane % seqs == pick_row
    bias[...] = lax.dot_general(
        masks, jnp.where(pick, 1.0, 0.0).astype(jnp.bfloat16), (((0,), (0,)), ((), ())),
        preferred_element_type=jnp.float32,
    )

    def fold(x, op):
        return op(x.reshape(x.shape[0] // 8, 8, x.shape[1]), axis=0)

    def score(order, part, top):
        for b in range(part * cut, (part + 1) * cut, STEP):
            got = jnp.dot(
                kbuf[order, b : b + STEP, :], qt[order], preferred_element_type=jnp.float32
            ) + bias[b : b + STEP, :]
            sbuf[order, b : b + STEP, :] = got
            high = fold(got, jnp.max)
            top = high if top is None else jnp.maximum(top, high)
        return top

    def weigh(order, top):
        m = jnp.max(top, axis=0, keepdims=True)
        total = None
        for b in range(0, slots, STEP):
            w = jnp.exp2((sbuf[order, b : b + STEP, :] - m) * SHIFT)
            pbuf[order, b : b + STEP, :] = w.astype(jnp.bfloat16)
            part = fold(w, jnp.sum)
            total = part if total is None else total + part
        return jnp.concatenate([m, jnp.sum(total, axis=0, keepdims=True)], axis=0)

    def gather(order, j):
        full = lax.dot_general(
            pbuf[order], vbuf[order * CHUNKS + j], (((0,), (0,)), ((), ())), preferred_element_type=jnp.float32
        )
        return jnp.concatenate(
            [full[(j * heads_each + e) * rows : (j * heads_each + e + 1) * rows, e * HD : (e + 1) * HD] for e in range(heads_each)],
            axis=0,
        )

    def remote(src, dst, ss, rs, device):
        return pltpu.make_async_remote_copy(
            src_ref=src, dst_ref=dst, send_sem=ss, recv_sem=rs, device_id={"seq": device}, device_id_type=MESH
        )

    def ml_to_partner():
        return remote(half_ml, peer_ml, hsm, hrm, partner)

    def num_to_partner(j):
        return remote(half_num.at[j], peer_num.at[j], hs.at[j], hr.at[j], partner)

    targets = [r * 2 + side for r in roots for side in range(2)]

    def ml_to_root(i):
        return remote(chip_ml.at[chip], chip_ml.at[chip], csm.at[i], crm.at[chip], targets[i] * 2 + core)

    def num_to_root(j, i):
        return remote(chip_num.at[j, chip], chip_num.at[j, chip], cs.at[j, i], cr.at[j, chip], targets[i] * 2 + core)

    def ml_from_chip(k):
        slot = (chip + k) % chips
        return remote(chip_ml.at[slot], chip_ml.at[slot], csm.at[0], crm.at[slot], slot * 2 + core)

    def num_from_chip(j, k):
        slot = (chip + k) % chips
        return remote(chip_num.at[j, slot], chip_num.at[j, slot], cs.at[j, 0], cr.at[j, slot], slot * 2 + core)

    def part_of(owner, j):
        return out.at[:, pl.ds(pl.multiple_of(owner * (CHUNKS * span) + j * span, span), span), :]

    def elsewhere(i, act):
        @pl.when(chip != targets[i])
        def _():
            act()

    k_copy(0).wait()
    top = score(0, 0, None)
    k_copy(1).wait()
    top = score(0, 1, top)
    k_copy(2).wait()
    own_top = score(1, 0, None)
    half_ml[...] = weigh(0, top)
    k_copy(3).wait()
    own_top = score(1, 1, own_top)
    for r in roots:
        @pl.when(plane == r)
        def _():
            pl.semaphore_wait(barrier, len(targets) + 2 * len(guests[r]))

    @pl.when(jnp.logical_not(is_root))
    def _():
        pl.semaphore_wait(barrier, 1 + len(targets))

    ml_to_partner().start()
    for j in range(CHUNKS):
        v_copy(j).wait()
    ml = weigh(1, own_top)
    for j in range(CHUNKS):
        half_num[j] = gather(0, j).astype(jnp.bfloat16)
        num_to_partner(j).start()

    v_copy(CHUNKS).wait()
    numers = [gather(1, 0)]
    ml_to_partner().wait_recv()
    other = peer_ml[...]
    top = jnp.maximum(ml[0:1], other[0:1])
    mine = jnp.exp2((ml[0:1] - top) * SHIFT)
    theirs = jnp.exp2((other[0:1] - top) * SHIFT)
    chip_ml[chip] = jnp.concatenate([top, mine * ml[1:2] + theirs * other[1:2]], axis=0)
    columns = jnp.transpose(jnp.concatenate([mine, theirs, jnp.zeros((6, lanes), jnp.float32)], axis=0))
    for i in range(len(targets)):
        elsewhere(i, lambda: ml_to_root(i).start())
    for j in range(1, CHUNKS):
        v_copy(CHUNKS + j).wait()
        numers.append(gather(1, j))
    for j in range(CHUNKS):
        num_to_partner(j).wait_recv()
        some = slice(j * block, (j + 1) * block)
        total = numers[j] * columns[some, 0:1] + peer_num[j].astype(jnp.float32) * columns[some, 1:2]
        chip_num[j, chip] = total.astype(jnp.bfloat16)
        for i in range(2):
            elsewhere(i, lambda: num_to_root(j, i).start())
    for j in range(CHUNKS):
        for i in range(2, len(targets)):
            elsewhere(i, lambda: num_to_root(j, i).start())

    @pl.when(is_root)
    def _():
        for k in range(1, chips):
            ml_from_chip(k).wait_recv()
        maxima = [chip_ml[i][0:1] for i in range(chips)]
        top = functools.reduce(jnp.maximum, maxima)
        factors = [jnp.exp2((m - top) * SHIFT) for m in maxima]
        denom = sum(f * chip_ml[i][1:2] for i, f in enumerate(factors))
        factors = [f / denom for f in factors]
        pad = -chips % 8
        if pad:
            factors = factors + [jnp.zeros((pad, lanes), jnp.float32)]
        columns = jnp.transpose(jnp.concatenate(factors, axis=0))
        for j in range(CHUNKS):
            for k in range(1, chips):
                num_from_chip(j, k).wait_recv()
            numer = None
            for i in range(chips):
                term = chip_num[j, i].astype(jnp.float32) * columns[j * block : (j + 1) * block, i : i + 1]
                numer = term if numer is None else numer + term
            attended = numer.astype(jnp.bfloat16)
            for e in range(heads_each):
                for t in range(2):
                    base = pl.multiple_of(core * (CHUNKS * span) + j * span + e * tile, tile)
                    out[t, pl.ds(base, tile), :] = attended[e * rows + t * tile : e * rows + (t + 1) * tile]
            remote(part_of(core, j), part_of(core, j), ps.at[j], pr.at[j], partner).start()
            for r in roots:
                if guests[r]:
                    @pl.when(plane == r)
                    def _():
                        for i, guest in enumerate(guests[r]):
                            for d in range(2):
                                device = (guest * 2 + y) * 2 + d
                                remote(part_of(core, j), part_of(core, j), fs.at[j, i, d], fr.at[j, core], device).start()
        for j in range(CHUNKS):
            remote(part_of(core, j), part_of(1 - core, j), ps.at[j], pr.at[j], partner).wait_recv()
        for j in range(CHUNKS):
            remote(part_of(core, j), part_of(core, j), ps.at[j], pr.at[j], partner).wait_send()
            for r in roots:
                if guests[r]:
                    @pl.when(plane == r)
                    def _():
                        for i, guest in enumerate(guests[r]):
                            for d in range(2):
                                device = (guest * 2 + y) * 2 + d
                                remote(part_of(core, j), part_of(core, j), fs.at[j, i, d], fr.at[j, core], device).wait_send()

    @pl.when(jnp.logical_not(is_root))
    def _():
        for j in range(CHUNKS):
            for d in range(2):
                remote(part_of(d, j), part_of(d, j), fs.at[j, 0, d], fr.at[j, d], server * 2 + d).wait_recv()

    ml_to_partner().wait_send()
    for j in range(CHUNKS):
        num_to_partner(j).wait_send()
    for i in range(len(targets)):
        elsewhere(i, lambda: ml_to_root(i).wait_send())
        for j in range(CHUNKS):
            elsewhere(i, lambda: num_to_root(j, i).wait_send())


def per_device(n, queries, cache_k, cache_v, context_len, slot_seq, slot_pos):
    slots = cache_k.shape[0]
    seqs = queries.shape[1]
    heads = queries.shape[2] // HD
    rows = 2 * seqs * heads // KVH
    heads_half = KVH // 2
    lanes = heads_half * rows
    block = lanes // CHUNKS
    chips = n // 2
    fans = 2 * len(root_planes(chips // 2))
    vmem = pl.BlockSpec(memory_space=pltpu.VMEM)
    dma = pltpu.SemaphoreType.DMA
    anywhere = pl.BlockSpec(memory_space=pltpu.HBM)
    attended = pl.pallas_call(
        functools.partial(kernel, n),
        out_shape=jax.ShapeDtypeStruct((2, heads * seqs, HD), jnp.bfloat16),
        in_specs=[anywhere] * 6,
        out_specs=vmem,
        scratch_shapes=[
            pltpu.SMEM((seqs,), jnp.int32),
            pltpu.VMEM(queries.shape, jnp.bfloat16),
            pltpu.VMEM((1, slots), jnp.int32),
            pltpu.VMEM((1, slots), jnp.int32),
            pltpu.VMEM((2, slots, heads_half * HD), jnp.bfloat16),
            pltpu.VMEM((2 * CHUNKS, slots, heads_half * HD // CHUNKS), jnp.bfloat16),
            pltpu.VMEM((KVH * rows, HD), jnp.float32),
            pltpu.VMEM((2, heads_half * HD, lanes), jnp.bfloat16),
            pltpu.VMEM((slots, lanes), jnp.float32),
            pltpu.VMEM((2, slots, lanes), jnp.float32),
            pltpu.VMEM((2, slots, lanes), jnp.bfloat16),
            pltpu.VMEM((CHUNKS, block, HD), jnp.bfloat16),
            pltpu.VMEM((2, lanes), jnp.float32),
            pltpu.VMEM((CHUNKS, block, HD), jnp.bfloat16),
            pltpu.VMEM((2, lanes), jnp.float32),
            pltpu.VMEM((CHUNKS, chips, block, HD), jnp.bfloat16),
            pltpu.VMEM((chips, 2, lanes), jnp.float32),
            dma((4,)), dma((2 * CHUNKS,)), dma((2 * CHUNKS,)),
            dma((CHUNKS,)), dma(()), dma((CHUNKS,)), dma(()),
            dma((CHUNKS, fans)), dma((fans,)), dma((CHUNKS, chips)), dma((chips,)),
            dma((CHUNKS,)), dma((CHUNKS,)),
            dma((CHUNKS, chips // 2, 2)), dma((CHUNKS, 2)),
        ],
        compiler_params=pltpu.CompilerParams(collective_id=0, has_side_effects=True, vmem_limit_bytes=LIMIT),
    )(*[
        pltpu.with_memory_space_constraint(x, pltpu.HBM)
        for x in (context_len, queries, cache_k, cache_v, slot_seq.reshape(1, slots), slot_pos.reshape(1, slots))
    ])
    steps = queries.shape[0]
    return attended.reshape(steps, heads, seqs, HD).transpose(0, 2, 1, 3).reshape(queries.shape)


def solution(mesh):
    return jax.shard_map(
        functools.partial(per_device, mesh.shape["seq"]),
        mesh=mesh,
        in_specs=(
            P(None, "parts", None),
            P(("parts", "seq"), None),
            P(("parts", "seq"), None),
            P("parts"),
            P(("parts", "seq")),
            P(("parts", "seq")),
        ),
        out_specs=P(None, "parts", None),
        check_vma=False,
    )
```

```python
import functools

import jax
import jax.numpy as jnp
from jax import lax
from jax.experimental import pallas as pl
from jax.experimental.pallas import tpu as pltpu
from jax.sharding import PartitionSpec as P

KVH = 8
HD = 128
CHUNKS = 2
STEP = 256
LIMIT = 24 << 20
SHIFT = HD ** (-0.5) * 1.4426950408889634
HIDDEN = -1e30
MESH = pl.DeviceIdType.MESH


def served_by(plane, planes):
    return (planes // 2) * ((4 * plane // planes + 2) // 3)


def root_planes(planes):
    return (0, planes // 2) if planes > 1 else (0,)


def kernel(
    n, ctx_hbm, q_hbm, k_hbm, v_hbm, seq_hbm, pos_hbm, out,
    ctx, q_ref, seq_ref, pos_ref, kbuf, vbuf, qf, qt, bias, sbuf, pbuf,
    half_num, half_ml, peer_num, peer_ml, chip_num, chip_ml,
    isem, ksem, vsem, hs, hsm, hr, hrm, cs, csm, cr, crm, ps, pr, fs, fr,
):
    me = lax.axis_index("seq")
    chips = n // 2
    planes = chips // 2
    core = me % 2
    chip = me // 2
    y = chip % 2
    plane = chip // 2
    roots = root_planes(planes)
    is_root = functools.reduce(lambda a, b: a | b, [plane == r for r in roots])
    partner = chip * 2 + (1 - core)
    server = served_by(plane, planes) * 2 + y
    guests = {r: [p for p in range(planes) if p not in roots and served_by(p, planes) == r] for r in roots}
    halves = (1 - core, core)
    slots = k_hbm.shape[0]
    heads_half = KVH // 2
    heads_each = heads_half // CHUNKS
    wide = heads_half * HD
    width = heads_each * HD
    group = q_ref.shape[2] // HD // KVH
    seqs = q_ref.shape[1]
    rows = 2 * seqs * group
    lanes = heads_half * rows
    block = heads_each * rows
    tile = group * seqs
    span = heads_each * tile
    cut = slots // CHUNKS

    barrier = pltpu.get_barrier_semaphore()

    def greet(device):
        pl.semaphore_signal(barrier, inc=1, device_id={"seq": device}, device_id_type=MESH)

    inputs = []
    for i, (src, dst) in enumerate(((q_hbm, q_ref), (seq_hbm, seq_ref), (pos_hbm, pos_ref), (ctx_hbm, ctx))):
        copy = pltpu.make_async_copy(src, dst, isem.at[i])
        copy.start()
        inputs.append(copy)

    def first_column(order):
        half = core * order + (1 - core) * (1 - order)
        return half * wide

    def k_copy(i):
        order, part = i // CHUNKS, i % CHUNKS
        some = pl.ds(pl.multiple_of(part * cut, cut), cut)
        columns = pl.ds(pl.multiple_of(first_column(order), wide), wide)
        return pltpu.make_async_copy(k_hbm.at[some, columns], kbuf.at[order, some], ksem.at[i])

    def v_copy(i):
        order, part = i // CHUNKS, i % CHUNKS
        columns = pl.ds(pl.multiple_of(first_column(order) + part * width, width), width)
        return pltpu.make_async_copy(v_hbm.at[:, columns], vbuf.at[i], vsem.at[i])

    def load_k(i, carry):
        k_copy(i).start()
        return carry

    def load_v(i, carry):
        v_copy(i).start()
        return carry

    lax.fori_loop(0, 2 * CHUNKS, load_k, 0)
    lax.fori_loop(0, 2 * CHUNKS, load_v, 0)

    greet(partner)

    @pl.when(is_root)
    def _():
        for k in range(1, chips):
            greet((chip + k) % chips * 2 + core)

    @pl.when(jnp.logical_not(is_root))
    def _():
        for d in range(2):
            greet(server * 2 + d)

    for copy in inputs:
        copy.wait()

    for t in range(2):
        for head in range(KVH * group):
            g, h = head // group, head % group
            base = g * rows + t * group * seqs + h * seqs
            qf[base : base + seqs, :] = q_ref[t, :, head * HD : (head + 1) * HD].astype(jnp.float32)

    column = lax.broadcasted_iota(jnp.int32, (HD, lanes), 1)
    for order in range(2):
        turned = jnp.transpose(qf[pl.ds(pl.multiple_of(halves[order] * lanes, lanes), lanes), :])
        for e in range(heads_half):
            qt[order, e * HD : (e + 1) * HD, :] = jnp.where(column // rows == e, turned, 0.0).astype(jnp.bfloat16)

    masks = []
    for t in range(2):
        for sq in range(seqs):
            allowed = (seq_ref[...] == sq) & (pos_ref[...] <= ctx[sq] - 2 + t)
            masks.append(jnp.where(allowed, 0.0, HIDDEN))
    pad = -len(masks) % 16
    masks = jnp.concatenate(masks + [jnp.zeros((pad, slots), jnp.float32)], axis=0).astype(jnp.bfloat16)
    pick_row = lax.broadcasted_iota(jnp.int32, (2 * seqs + pad, lanes), 0)
    pick_lane = lax.broadcasted_iota(jnp.int32, (2 * seqs + pad, lanes), 1) % rows
    pick = (pick_lane // tile) * seqs + pick_lane % seqs == pick_row
    bias[...] = lax.dot_general(
        masks, jnp.where(pick, 1.0, 0.0).astype(jnp.bfloat16), (((0,), (0,)), ((), ())),
        preferred_element_type=jnp.float32,
    )

    def fold(x, op):
        return op(x.reshape(x.shape[0] // 8, 8, x.shape[1]), axis=0)

    def score(order, part, top):
        for b in range(part * cut, (part + 1) * cut, STEP):
            got = jnp.dot(
                kbuf[order, b : b + STEP, :], qt[order], preferred_element_type=jnp.float32
            ) + bias[b : b + STEP, :]
            sbuf[order, b : b + STEP, :] = got
            high = fold(got, jnp.max)
            top = high if top is None else jnp.maximum(top, high)
        return top

    def weigh(order, top):
        m = jnp.max(top, axis=0, keepdims=True)
        total = None
        for b in range(0, slots, STEP):
            w = jnp.exp2((sbuf[order, b : b + STEP, :] - m) * SHIFT)
            pbuf[order, b : b + STEP, :] = w.astype(jnp.bfloat16)
            part = fold(w, jnp.sum)
            total = part if total is None else total + part
        return jnp.concatenate([m, jnp.sum(total, axis=0, keepdims=True)], axis=0)

    def gather(order, j):
        full = lax.dot_general(
            pbuf[order], vbuf[order * CHUNKS + j], (((0,), (0,)), ((), ())), preferred_element_type=jnp.float32
        )
        return jnp.concatenate(
            [full[(j * heads_each + e) * rows : (j * heads_each + e + 1) * rows, e * HD : (e + 1) * HD] for e in range(heads_each)],
            axis=0,
        )

    def remote(src, dst, ss, rs, device):
        return pltpu.make_async_remote_copy(
            src_ref=src, dst_ref=dst, send_sem=ss, recv_sem=rs, device_id={"seq": device}, device_id_type=MESH
        )

    def ml_to_partner():
        return remote(half_ml, peer_ml, hsm, hrm, partner)

    def num_to_partner(j):
        return remote(half_num.at[j], peer_num.at[j], hs.at[j], hr.at[j], partner)

    targets = [r * 2 + side for r in roots for side in range(2)]

    def ml_to_root(i):
        return remote(chip_ml.at[chip], chip_ml.at[chip], csm.at[i], crm.at[chip], targets[i] * 2 + core)

    def num_to_root(j, i):
        return remote(chip_num.at[j, chip], chip_num.at[j, chip], cs.at[j, i], cr.at[j, chip], targets[i] * 2 + core)

    def ml_from_chip(k):
        slot = (chip + k) % chips
        return remote(chip_ml.at[slot], chip_ml.at[slot], csm.at[0], crm.at[slot], slot * 2 + core)

    def num_from_chip(j, k):
        slot = (chip + k) % chips
        return remote(chip_num.at[j, slot], chip_num.at[j, slot], cs.at[j, 0], cr.at[j, slot], slot * 2 + core)

    def part_of(owner, j):
        return out.at[:, pl.ds(pl.multiple_of(owner * (CHUNKS * span) + j * span, span), span), :]

    def elsewhere(i, act):
        @pl.when(chip != targets[i])
        def _():
            act()

    k_copy(0).wait()
    top = score(0, 0, None)
    k_copy(1).wait()
    top = score(0, 1, top)
    for i in range(CHUNKS, 2 * CHUNKS):
        k_copy(i).wait()
    half_ml[...] = weigh(0, top)
    own_top = None
    for part in range(CHUNKS):
        own_top = score(1, part, own_top)
    for r in roots:
        @pl.when(plane == r)
        def _():
            pl.semaphore_wait(barrier, len(targets) + 2 * len(guests[r]))

    @pl.when(jnp.logical_not(is_root))
    def _():
        pl.semaphore_wait(barrier, 1 + len(targets))

    ml_to_partner().start()
    for j in range(CHUNKS):
        v_copy(j).wait()
    ml = weigh(1, own_top)
    for j in range(CHUNKS):
        half_num[j] = gather(0, j).astype(jnp.bfloat16)
        num_to_partner(j).start()

    for j in range(CHUNKS):
        v_copy(CHUNKS + j).wait()
    numers = [gather(1, j) for j in range(CHUNKS)]
    ml_to_partner().wait_recv()
    other = peer_ml[...]
    top = jnp.maximum(ml[0:1], other[0:1])
    mine = jnp.exp2((ml[0:1] - top) * SHIFT)
    theirs = jnp.exp2((other[0:1] - top) * SHIFT)
    chip_ml[chip] = jnp.concatenate([top, mine * ml[1:2] + theirs * other[1:2]], axis=0)
    columns = jnp.transpose(jnp.concatenate([mine, theirs, jnp.zeros((6, lanes), jnp.float32)], axis=0))
    for i in range(len(targets)):
        elsewhere(i, lambda: ml_to_root(i).start())
    for j in range(CHUNKS):
        num_to_partner(j).wait_recv()
        some = slice(j * block, (j + 1) * block)
        total = numers[j] * columns[some, 0:1] + peer_num[j].astype(jnp.float32) * columns[some, 1:2]
        chip_num[j, chip] = total.astype(jnp.bfloat16)
        elsewhere(0, lambda: num_to_root(j, 0).start())
    @pl.when(core == 1)
    def _():
        for j in range(CHUNKS):
            elsewhere(0, lambda: num_to_root(j, 0).wait_send())

    for i in (2, 3, 1):
        for j in range(CHUNKS):
            elsewhere(i, lambda: num_to_root(j, i).start())

    @pl.when(is_root)
    def _():
        for k in range(1, chips):
            ml_from_chip(k).wait_recv()
        maxima = [chip_ml[i][0:1] for i in range(chips)]
        top = functools.reduce(jnp.maximum, maxima)
        factors = [jnp.exp2((m - top) * SHIFT) for m in maxima]
        denom = sum(f * chip_ml[i][1:2] for i, f in enumerate(factors))
        factors = [f / denom for f in factors]
        pad = -chips % 8
        if pad:
            factors = factors + [jnp.zeros((pad, lanes), jnp.float32)]
        columns = jnp.transpose(jnp.concatenate(factors, axis=0))
        for j in range(CHUNKS):
            for k in range(1, chips):
                num_from_chip(j, k).wait_recv()
            numer = None
            for i in range(chips):
                term = chip_num[j, i].astype(jnp.float32) * columns[j * block : (j + 1) * block, i : i + 1]
                numer = term if numer is None else numer + term
            attended = numer.astype(jnp.bfloat16)
            for e in range(heads_each):
                for t in range(2):
                    base = pl.multiple_of(core * (CHUNKS * span) + j * span + e * tile, tile)
                    out[t, pl.ds(base, tile), :] = attended[e * rows + t * tile : e * rows + (t + 1) * tile]
            remote(part_of(core, j), part_of(core, j), ps.at[j], pr.at[j], partner).start()
            for r in roots:
                if guests[r]:
                    @pl.when(plane == r)
                    def _():
                        for i, guest in enumerate(guests[r]):
                            for d in range(2):
                                device = (guest * 2 + y) * 2 + d
                                remote(part_of(core, j), part_of(core, j), fs.at[j, i, d], fr.at[j, core], device).start()
        for j in range(CHUNKS):
            remote(part_of(core, j), part_of(1 - core, j), ps.at[j], pr.at[j], partner).wait_recv()
        for j in range(CHUNKS):
            remote(part_of(core, j), part_of(core, j), ps.at[j], pr.at[j], partner).wait_send()
            for r in roots:
                if guests[r]:
                    @pl.when(plane == r)
                    def _():
                        for i, guest in enumerate(guests[r]):
                            for d in range(2):
                                device = (guest * 2 + y) * 2 + d
                                remote(part_of(core, j), part_of(core, j), fs.at[j, i, d], fr.at[j, core], device).wait_send()

    @pl.when(jnp.logical_not(is_root))
    def _():
        for j in range(CHUNKS):
            for d in range(2):
                remote(part_of(d, j), part_of(d, j), fs.at[j, 0, d], fr.at[j, d], server * 2 + d).wait_recv()

    ml_to_partner().wait_send()
    for j in range(CHUNKS):
        num_to_partner(j).wait_send()
    for i in range(len(targets)):
        elsewhere(i, lambda: ml_to_root(i).wait_send())
        for j in range(CHUNKS):
            if i:
                elsewhere(i, lambda: num_to_root(j, i).wait_send())
            else:
                @pl.when(core == 0)
                def _():
                    elsewhere(0, lambda: num_to_root(j, 0).wait_send())


def per_device(n, queries, cache_k, cache_v, context_len, slot_seq, slot_pos):
    slots = cache_k.shape[0]
    seqs = queries.shape[1]
    heads = queries.shape[2] // HD
    rows = 2 * seqs * heads // KVH
    heads_half = KVH // 2
    lanes = heads_half * rows
    block = lanes // CHUNKS
    chips = n // 2
    fans = 2 * len(root_planes(chips // 2))
    vmem = pl.BlockSpec(memory_space=pltpu.VMEM)
    dma = pltpu.SemaphoreType.DMA
    anywhere = pl.BlockSpec(memory_space=pltpu.HBM)
    attended = pl.pallas_call(
        functools.partial(kernel, n),
        out_shape=jax.ShapeDtypeStruct((2, heads * seqs, HD), jnp.bfloat16),
        in_specs=[anywhere] * 6,
        out_specs=vmem,
        scratch_shapes=[
            pltpu.SMEM((seqs,), jnp.int32),
            pltpu.VMEM(queries.shape, jnp.bfloat16),
            pltpu.VMEM((1, slots), jnp.int32),
            pltpu.VMEM((1, slots), jnp.int32),
            pltpu.VMEM((2, slots, heads_half * HD), jnp.bfloat16),
            pltpu.VMEM((2 * CHUNKS, slots, heads_half * HD // CHUNKS), jnp.bfloat16),
            pltpu.VMEM((KVH * rows, HD), jnp.float32),
            pltpu.VMEM((2, heads_half * HD, lanes), jnp.bfloat16),
            pltpu.VMEM((slots, lanes), jnp.float32),
            pltpu.VMEM((2, slots, lanes), jnp.float32),
            pltpu.VMEM((2, slots, lanes), jnp.bfloat16),
            pltpu.VMEM((CHUNKS, block, HD), jnp.bfloat16),
            pltpu.VMEM((2, lanes), jnp.float32),
            pltpu.VMEM((CHUNKS, block, HD), jnp.bfloat16),
            pltpu.VMEM((2, lanes), jnp.float32),
            pltpu.VMEM((CHUNKS, chips, block, HD), jnp.bfloat16),
            pltpu.VMEM((chips, 2, lanes), jnp.float32),
            dma((4,)), dma((2 * CHUNKS,)), dma((2 * CHUNKS,)),
            dma((CHUNKS,)), dma(()), dma((CHUNKS,)), dma(()),
            dma((CHUNKS, fans)), dma((fans,)), dma((CHUNKS, chips)), dma((chips,)),
            dma((CHUNKS,)), dma((CHUNKS,)),
            dma((CHUNKS, chips // 2, 2)), dma((CHUNKS, 2)),
        ],
        compiler_params=pltpu.CompilerParams(collective_id=0, has_side_effects=True, vmem_limit_bytes=LIMIT),
    )(*[
        pltpu.with_memory_space_constraint(x, pltpu.HBM)
        for x in (context_len, queries, cache_k, cache_v, slot_seq.reshape(1, slots), slot_pos.reshape(1, slots))
    ])
    steps = queries.shape[0]
    return attended.reshape(steps, heads, seqs, HD).transpose(0, 2, 1, 3).reshape(queries.shape)


def solution(mesh):
    return jax.shard_map(
        functools.partial(per_device, mesh.shape["seq"]),
        mesh=mesh,
        in_specs=(
            P(None, "parts", None),
            P(("parts", "seq"), None),
            P(("parts", "seq"), None),
            P("parts"),
            P(("parts", "seq")),
            P(("parts", "seq")),
        ),
        out_specs=P(None, "parts", None),
        check_vma=False,
    )
```

```python
import functools

import jax
import jax.numpy as jnp
from jax import lax
from jax.experimental import pallas as pl
from jax.experimental.pallas import tpu as pltpu
from jax.sharding import PartitionSpec as P

KVH = 8
HD = 128
CHUNKS = 2
STEP = 256
LIMIT = 24 << 20
SHIFT = HD ** (-0.5) * 1.4426950408889634
HIDDEN = -1e30
MESH = pl.DeviceIdType.MESH


def served_by(plane, planes):
    return (planes // 2) * ((4 * plane // planes + 2) // 3)


def root_planes(planes):
    return (0, planes // 2) if planes > 1 else (0,)


def kernel(
    n, ctx_hbm, q_hbm, k_hbm, v_hbm, seq_hbm, pos_hbm, out,
    ctx, q_ref, seq_ref, pos_ref, kbuf, vbuf, qf, qt, bias, sbuf, pbuf,
    half_num, half_ml, peer_num, peer_ml, chip_num, chip_ml,
    isem, ksem, vsem, hs, hsm, hr, hrm, cs, csm, cr, crm, ps, pr, fs, fr,
):
    me = lax.axis_index("seq")
    chips = n // 2
    planes = chips // 2
    core = me % 2
    chip = me // 2
    y = chip % 2
    plane = chip // 2
    roots = root_planes(planes)
    is_root = functools.reduce(lambda a, b: a | b, [plane == r for r in roots])
    partner = chip * 2 + (1 - core)
    server = served_by(plane, planes) * 2 + y
    guests = {r: [p for p in range(planes) if p not in roots and served_by(p, planes) == r] for r in roots}
    halves = (1 - core, core)
    slots = k_hbm.shape[0]
    heads_half = KVH // 2
    heads_each = heads_half // CHUNKS
    wide = heads_half * HD
    width = heads_each * HD
    group = q_ref.shape[2] // HD // KVH
    seqs = q_ref.shape[1]
    rows = 2 * seqs * group
    lanes = heads_half * rows
    block = heads_each * rows
    tile = group * seqs
    span = heads_each * tile
    cut = slots // CHUNKS

    barrier = pltpu.get_barrier_semaphore()

    def greet(device):
        pl.semaphore_signal(barrier, inc=1, device_id={"seq": device}, device_id_type=MESH)

    inputs = []
    for i, (src, dst) in enumerate(((q_hbm, q_ref), (seq_hbm, seq_ref), (pos_hbm, pos_ref), (ctx_hbm, ctx))):
        copy = pltpu.make_async_copy(src, dst, isem.at[i])
        copy.start()
        inputs.append(copy)

    def first_column(order):
        half = core * order + (1 - core) * (1 - order)
        return half * wide

    def k_copy(i):
        order, part = i // CHUNKS, i % CHUNKS
        some = pl.ds(pl.multiple_of(part * cut, cut), cut)
        columns = pl.ds(pl.multiple_of(first_column(order), wide), wide)
        return pltpu.make_async_copy(k_hbm.at[some, columns], kbuf.at[order, some], ksem.at[i])

    def v_copy(i):
        order, part = i // CHUNKS, i % CHUNKS
        columns = pl.ds(pl.multiple_of(first_column(order) + part * width, width), width)
        return pltpu.make_async_copy(v_hbm.at[:, columns], vbuf.at[i], vsem.at[i])

    def load_k(i, carry):
        k_copy(i).start()
        return carry

    def load_v(i, carry):
        v_copy(i).start()
        return carry

    lax.fori_loop(0, 3, load_k, 0)
    lax.fori_loop(0, 2, load_v, 0)
    k_copy(3).start()
    lax.fori_loop(2, 4, load_v, 0)

    greet(partner)

    @pl.when(is_root)
    def _():
        for k in range(1, chips):
            greet((chip + k) % chips * 2 + core)

    @pl.when(jnp.logical_not(is_root))
    def _():
        for d in range(2):
            greet(server * 2 + d)

    for copy in inputs:
        copy.wait()

    for t in range(2):
        for head in range(KVH * group):
            g, h = head // group, head % group
            base = g * rows + t * group * seqs + h * seqs
            qf[base : base + seqs, :] = q_ref[t, :, head * HD : (head + 1) * HD].astype(jnp.float32)

    column = lax.broadcasted_iota(jnp.int32, (HD, lanes), 1)
    for order in range(2):
        turned = jnp.transpose(qf[pl.ds(pl.multiple_of(halves[order] * lanes, lanes), lanes), :])
        for e in range(heads_half):
            qt[order, e * HD : (e + 1) * HD, :] = jnp.where(column // rows == e, turned, 0.0).astype(jnp.bfloat16)

    masks = []
    for t in range(2):
        for sq in range(seqs):
            allowed = (seq_ref[...] == sq) & (pos_ref[...] <= ctx[sq] - 2 + t)
            masks.append(jnp.where(allowed, 0.0, HIDDEN))
    pad = -len(masks) % 16
    masks = jnp.concatenate(masks + [jnp.zeros((pad, slots), jnp.float32)], axis=0).astype(jnp.bfloat16)
    pick_row = lax.broadcasted_iota(jnp.int32, (2 * seqs + pad, lanes), 0)
    pick_lane = lax.broadcasted_iota(jnp.int32, (2 * seqs + pad, lanes), 1) % rows
    pick = (pick_lane // tile) * seqs + pick_lane % seqs == pick_row
    bias[...] = lax.dot_general(
        masks, jnp.where(pick, 1.0, 0.0).astype(jnp.bfloat16), (((0,), (0,)), ((), ())),
        preferred_element_type=jnp.float32,
    )

    def fold(x, op):
        return op(x.reshape(x.shape[0] // 8, 8, x.shape[1]), axis=0)

    def score(order, part, top):
        for b in range(part * cut, (part + 1) * cut, STEP):
            got = jnp.dot(
                kbuf[order, b : b + STEP, :], qt[order], preferred_element_type=jnp.float32
            ) + bias[b : b + STEP, :]
            sbuf[order, b : b + STEP, :] = got
            high = fold(got, jnp.max)
            top = high if top is None else jnp.maximum(top, high)
        return top

    def weigh(order, top):
        m = jnp.max(top, axis=0, keepdims=True)
        total = None
        for b in range(0, slots, STEP):
            w = jnp.exp2((sbuf[order, b : b + STEP, :] - m) * SHIFT)
            pbuf[order, b : b + STEP, :] = w.astype(jnp.bfloat16)
            part = fold(w, jnp.sum)
            total = part if total is None else total + part
        return jnp.concatenate([m, jnp.sum(total, axis=0, keepdims=True)], axis=0)

    def gather(order, j):
        full = lax.dot_general(
            pbuf[order], vbuf[order * CHUNKS + j], (((0,), (0,)), ((), ())), preferred_element_type=jnp.float32
        )
        return jnp.concatenate(
            [full[(j * heads_each + e) * rows : (j * heads_each + e + 1) * rows, e * HD : (e + 1) * HD] for e in range(heads_each)],
            axis=0,
        )

    def remote(src, dst, ss, rs, device):
        return pltpu.make_async_remote_copy(
            src_ref=src, dst_ref=dst, send_sem=ss, recv_sem=rs, device_id={"seq": device}, device_id_type=MESH
        )

    def ml_to_partner():
        return remote(half_ml, peer_ml, hsm, hrm, partner)

    def num_to_partner(j):
        return remote(half_num.at[j], peer_num.at[j], hs.at[j], hr.at[j], partner)

    targets = [r * 2 + side for r in roots for side in range(2)]

    def ml_to_root(i):
        return remote(chip_ml.at[chip], chip_ml.at[chip], csm.at[i], crm.at[chip], targets[i] * 2 + core)

    def num_to_root(j, i):
        return remote(chip_num.at[j, chip], chip_num.at[j, chip], cs.at[j, i], cr.at[j, chip], targets[i] * 2 + core)

    def ml_from_chip(k):
        slot = (chip + k) % chips
        return remote(chip_ml.at[slot], chip_ml.at[slot], csm.at[0], crm.at[slot], slot * 2 + core)

    def num_from_chip(j, k):
        slot = (chip + k) % chips
        return remote(chip_num.at[j, slot], chip_num.at[j, slot], cs.at[j, 0], cr.at[j, slot], slot * 2 + core)

    def part_of(owner, j):
        return out.at[:, pl.ds(pl.multiple_of(owner * (CHUNKS * span) + j * span, span), span), :]

    def elsewhere(i, act):
        @pl.when(chip != targets[i])
        def _():
            act()

    k_copy(0).wait()
    top = score(0, 0, None)
    k_copy(1).wait()
    top = score(0, 1, top)
    k_copy(2).wait()
    half_ml[...] = weigh(0, top)
    own_top = score(1, 0, None)
    for r in roots:
        @pl.when(plane == r)
        def _():
            pl.semaphore_wait(barrier, len(targets) + 2 * len(guests[r]))

    @pl.when(jnp.logical_not(is_root))
    def _():
        pl.semaphore_wait(barrier, 1 + len(targets))

    ml_to_partner().start()
    for j in range(CHUNKS):
        v_copy(j).wait()
    for j in range(CHUNKS):
        half_num[j] = gather(0, j).astype(jnp.bfloat16)
    for j in range(CHUNKS):
        num_to_partner(j).start()
    k_copy(3).wait()
    own_top = score(1, 1, own_top)
    ml = weigh(1, own_top)
    ml_to_partner().wait_recv()
    other = peer_ml[...]
    top = jnp.maximum(ml[0:1], other[0:1])
    mine = jnp.exp2((ml[0:1] - top) * SHIFT)
    theirs = jnp.exp2((other[0:1] - top) * SHIFT)
    chip_ml[chip] = jnp.concatenate([top, mine * ml[1:2] + theirs * other[1:2]], axis=0)
    columns = jnp.transpose(jnp.concatenate([mine, theirs, jnp.zeros((6, lanes), jnp.float32)], axis=0))
    for i in range(len(targets)):
        elsewhere(i, lambda: ml_to_root(i).start())
    for j in range(CHUNKS):
        v_copy(CHUNKS + j).wait()
    numers = [gather(1, j) for j in range(CHUNKS)]
    for j in range(CHUNKS):
        num_to_partner(j).wait_recv()
        some = slice(j * block, (j + 1) * block)
        total = numers[j] * columns[some, 0:1] + peer_num[j].astype(jnp.float32) * columns[some, 1:2]
        chip_num[j, chip] = total.astype(jnp.bfloat16)
        elsewhere(0, lambda: num_to_root(j, 0).start())
    @pl.when(core == 1)
    def _():
        for j in range(CHUNKS):
            elsewhere(0, lambda: num_to_root(j, 0).wait_send())

    for i in (2, 3, 1):
        for j in range(CHUNKS):
            elsewhere(i, lambda: num_to_root(j, i).start())

    @pl.when(is_root)
    def _():
        for k in range(1, chips):
            ml_from_chip(k).wait_recv()
        maxima = [chip_ml[i][0:1] for i in range(chips)]
        top = functools.reduce(jnp.maximum, maxima)
        factors = [jnp.exp2((m - top) * SHIFT) for m in maxima]
        denom = sum(f * chip_ml[i][1:2] for i, f in enumerate(factors))
        factors = [f / denom for f in factors]
        pad = -chips % 8
        if pad:
            factors = factors + [jnp.zeros((pad, lanes), jnp.float32)]
        columns = jnp.transpose(jnp.concatenate(factors, axis=0))
        for j in range(CHUNKS):
            for k in range(1, chips):
                num_from_chip(j, k).wait_recv()
            numer = None
            for i in range(chips):
                term = chip_num[j, i].astype(jnp.float32) * columns[j * block : (j + 1) * block, i : i + 1]
                numer = term if numer is None else numer + term
            attended = numer.astype(jnp.bfloat16)
            for e in range(heads_each):
                for t in range(2):
                    base = pl.multiple_of(core * (CHUNKS * span) + j * span + e * tile, tile)
                    out[t, pl.ds(base, tile), :] = attended[e * rows + t * tile : e * rows + (t + 1) * tile]
            remote(part_of(core, j), part_of(core, j), ps.at[j], pr.at[j], partner).start()
            for r in roots:
                if guests[r]:
                    @pl.when(plane == r)
                    def _():
                        for i, guest in enumerate(guests[r]):
                            for d in range(2):
                                device = (guest * 2 + y) * 2 + d
                                remote(part_of(core, j), part_of(core, j), fs.at[j, i, d], fr.at[j, core], device).start()
        for j in range(CHUNKS):
            remote(part_of(core, j), part_of(1 - core, j), ps.at[j], pr.at[j], partner).wait_recv()
        for j in range(CHUNKS):
            remote(part_of(core, j), part_of(core, j), ps.at[j], pr.at[j], partner).wait_send()
            for r in roots:
                if guests[r]:
                    @pl.when(plane == r)
                    def _():
                        for i, guest in enumerate(guests[r]):
                            for d in range(2):
                                device = (guest * 2 + y) * 2 + d
                                remote(part_of(core, j), part_of(core, j), fs.at[j, i, d], fr.at[j, core], device).wait_send()

    @pl.when(jnp.logical_not(is_root))
    def _():
        for j in range(CHUNKS):
            for d in range(2):
                remote(part_of(d, j), part_of(d, j), fs.at[j, 0, d], fr.at[j, d], server * 2 + d).wait_recv()

    ml_to_partner().wait_send()
    for j in range(CHUNKS):
        num_to_partner(j).wait_send()
    for i in range(len(targets)):
        elsewhere(i, lambda: ml_to_root(i).wait_send())
        for j in range(CHUNKS):
            if i:
                elsewhere(i, lambda: num_to_root(j, i).wait_send())
            else:
                @pl.when(core == 0)
                def _():
                    elsewhere(0, lambda: num_to_root(j, 0).wait_send())


def per_device(n, queries, cache_k, cache_v, context_len, slot_seq, slot_pos):
    slots = cache_k.shape[0]
    seqs = queries.shape[1]
    heads = queries.shape[2] // HD
    rows = 2 * seqs * heads // KVH
    heads_half = KVH // 2
    lanes = heads_half * rows
    block = lanes // CHUNKS
    chips = n // 2
    fans = 2 * len(root_planes(chips // 2))
    vmem = pl.BlockSpec(memory_space=pltpu.VMEM)
    dma = pltpu.SemaphoreType.DMA
    anywhere = pl.BlockSpec(memory_space=pltpu.HBM)
    attended = pl.pallas_call(
        functools.partial(kernel, n),
        out_shape=jax.ShapeDtypeStruct((2, heads * seqs, HD), jnp.bfloat16),
        in_specs=[anywhere] * 6,
        out_specs=vmem,
        scratch_shapes=[
            pltpu.SMEM((seqs,), jnp.int32),
            pltpu.VMEM(queries.shape, jnp.bfloat16),
            pltpu.VMEM((1, slots), jnp.int32),
            pltpu.VMEM((1, slots), jnp.int32),
            pltpu.VMEM((2, slots, heads_half * HD), jnp.bfloat16),
            pltpu.VMEM((2 * CHUNKS, slots, heads_half * HD // CHUNKS), jnp.bfloat16),
            pltpu.VMEM((KVH * rows, HD), jnp.float32),
            pltpu.VMEM((2, heads_half * HD, lanes), jnp.bfloat16),
            pltpu.VMEM((slots, lanes), jnp.float32),
            pltpu.VMEM((2, slots, lanes), jnp.float32),
            pltpu.VMEM((2, slots, lanes), jnp.bfloat16),
            pltpu.VMEM((CHUNKS, block, HD), jnp.bfloat16),
            pltpu.VMEM((2, lanes), jnp.float32),
            pltpu.VMEM((CHUNKS, block, HD), jnp.bfloat16),
            pltpu.VMEM((2, lanes), jnp.float32),
            pltpu.VMEM((CHUNKS, chips, block, HD), jnp.bfloat16),
            pltpu.VMEM((chips, 2, lanes), jnp.float32),
            dma((4,)), dma((2 * CHUNKS,)), dma((2 * CHUNKS,)),
            dma((CHUNKS,)), dma(()), dma((CHUNKS,)), dma(()),
            dma((CHUNKS, fans)), dma((fans,)), dma((CHUNKS, chips)), dma((chips,)),
            dma((CHUNKS,)), dma((CHUNKS,)),
            dma((CHUNKS, chips // 2, 2)), dma((CHUNKS, 2)),
        ],
        compiler_params=pltpu.CompilerParams(collective_id=0, has_side_effects=True, vmem_limit_bytes=LIMIT),
    )(*[
        pltpu.with_memory_space_constraint(x, pltpu.HBM)
        for x in (context_len, queries, cache_k, cache_v, slot_seq.reshape(1, slots), slot_pos.reshape(1, slots))
    ])
    steps = queries.shape[0]
    return attended.reshape(steps, heads, seqs, HD).transpose(0, 2, 1, 3).reshape(queries.shape)


def solution(mesh):
    return jax.shard_map(
        functools.partial(per_device, mesh.shape["seq"]),
        mesh=mesh,
        in_specs=(
            P(None, "parts", None),
            P(("parts", "seq"), None),
            P(("parts", "seq"), None),
            P("parts"),
            P(("parts", "seq")),
            P(("parts", "seq")),
        ),
        out_specs=P(None, "parts", None),
        check_vma=False,
    )
```

```python
import functools

import jax
import jax.numpy as jnp
from jax import lax
from jax.experimental import pallas as pl
from jax.experimental.pallas import tpu as pltpu
from jax.sharding import PartitionSpec as P

KVH = 8
HD = 128
CHUNKS = 2
STEP = 256
LIMIT = 24 << 20
SHIFT = HD ** (-0.5) * 1.4426950408889634
HIDDEN = -1e30
MESH = pl.DeviceIdType.MESH


def kernel(
    n, ctx_hbm, q_hbm, k_hbm, v_hbm, seq_hbm, pos_hbm, out,
    ctx, q_ref, seq_ref, pos_ref, kbuf, vbuf, qf, qt, bias, sbuf, pbuf,
    half_num, half_ml, peer_num, peer_ml, chip_num, chip_ml,
    isem, ksem, vsem, hs, hsm, hr, hrm, cs, csm, cr, crm, ps, pr, fs, fr,
):
    me = lax.axis_index("seq")
    chips = n // 2
    planes = chips // 2
    core = me % 2
    chip = me // 2
    y = chip % 2
    plane = chip // 2
    middle = planes // 2
    first, central = plane == 0, plane == middle
    guests = [p for p in range(planes) if p not in (0, middle)]
    guest = jnp.logical_not(first | central)
    partner = chip * 2 + (1 - core)
    across = (plane * 2 + (1 - y)) * 2
    halves = (1 - core, core)
    slots = k_hbm.shape[0]
    heads_half = KVH // 2
    heads_each = heads_half // CHUNKS
    wide = heads_half * HD
    width = heads_each * HD
    group = q_ref.shape[2] // HD // KVH
    seqs = q_ref.shape[1]
    rows = 2 * seqs * group
    lanes = heads_half * rows
    block = heads_each * rows
    tile = group * seqs
    span = heads_each * tile
    cut = slots // CHUNKS

    barrier = pltpu.get_barrier_semaphore()

    def greet(device):
        pl.semaphore_signal(barrier, inc=1, device_id={"seq": device}, device_id_type=MESH)

    inputs = []
    for i, (src, dst) in enumerate(((q_hbm, q_ref), (seq_hbm, seq_ref), (pos_hbm, pos_ref), (ctx_hbm, ctx))):
        copy = pltpu.make_async_copy(src, dst, isem.at[i])
        copy.start()
        inputs.append(copy)

    def first_column(order):
        half = core * order + (1 - core) * (1 - order)
        return half * wide

    def k_copy(i):
        order, part = i // CHUNKS, i % CHUNKS
        some = pl.ds(pl.multiple_of(part * cut, cut), cut)
        columns = pl.ds(pl.multiple_of(first_column(order), wide), wide)
        return pltpu.make_async_copy(k_hbm.at[some, columns], kbuf.at[order, some], ksem.at[i])

    def v_copy(i):
        order, part = i // CHUNKS, i % CHUNKS
        columns = pl.ds(pl.multiple_of(first_column(order) + part * width, width), width)
        return pltpu.make_async_copy(v_hbm.at[:, columns], vbuf.at[i], vsem.at[i])

    def load_k(i, carry):
        k_copy(i).start()
        return carry

    def load_v(i, carry):
        v_copy(i).start()
        return carry

    lax.fori_loop(0, 3, load_k, 0)
    lax.fori_loop(0, 2, load_v, 0)
    k_copy(3).start()
    lax.fori_loop(2, 4, load_v, 0)

    greet(partner)

    @pl.when(first | central)
    def _():
        for k in range(1, chips):
            greet((chip + k) % chips * 2 + core)

    @pl.when(central)
    def _():
        greet(across + (1 - core))

    @pl.when(guest)
    def _():
        for d in range(4):
            greet(middle * 4 + d)

    for copy in inputs:
        copy.wait()

    for t in range(2):
        for head in range(KVH * group):
            g, h = head // group, head % group
            base = g * rows + t * group * seqs + h * seqs
            qf[base : base + seqs, :] = q_ref[t, :, head * HD : (head + 1) * HD].astype(jnp.float32)

    column = lax.broadcasted_iota(jnp.int32, (HD, lanes), 1)
    for order in range(2):
        turned = jnp.transpose(qf[pl.ds(pl.multiple_of(halves[order] * lanes, lanes), lanes), :])
        for e in range(heads_half):
            qt[order, e * HD : (e + 1) * HD, :] = jnp.where(column // rows == e, turned, 0.0).astype(jnp.bfloat16)

    masks = []
    for t in range(2):
        for sq in range(seqs):
            allowed = (seq_ref[...] == sq) & (pos_ref[...] <= ctx[sq] - 2 + t)
            masks.append(jnp.where(allowed, 0.0, HIDDEN))
    pad = -len(masks) % 16
    masks = jnp.concatenate(masks + [jnp.zeros((pad, slots), jnp.float32)], axis=0).astype(jnp.bfloat16)
    pick_row = lax.broadcasted_iota(jnp.int32, (2 * seqs + pad, lanes), 0)
    pick_lane = lax.broadcasted_iota(jnp.int32, (2 * seqs + pad, lanes), 1) % rows
    pick = (pick_lane // tile) * seqs + pick_lane % seqs == pick_row
    bias[...] = lax.dot_general(
        masks, jnp.where(pick, 1.0, 0.0).astype(jnp.bfloat16), (((0,), (0,)), ((), ())),
        preferred_element_type=jnp.float32,
    )

    def fold(x, op):
        return op(x.reshape(x.shape[0] // 8, 8, x.shape[1]), axis=0)

    def score(order, part, top):
        for b in range(part * cut, (part + 1) * cut, STEP):
            got = jnp.dot(
                kbuf[order, b : b + STEP, :], qt[order], preferred_element_type=jnp.float32
            ) + bias[b : b + STEP, :]
            sbuf[order, b : b + STEP, :] = got
            high = fold(got, jnp.max)
            top = high if top is None else jnp.maximum(top, high)
        return top

    def weigh(order, top):
        m = jnp.max(top, axis=0, keepdims=True)
        total = None
        for b in range(0, slots, STEP):
            w = jnp.exp2((sbuf[order, b : b + STEP, :] - m) * SHIFT)
            pbuf[order, :, b : b + STEP] = jnp.transpose(w.astype(jnp.bfloat16))
            part = fold(w, jnp.sum)
            total = part if total is None else total + part
        return jnp.concatenate([m, jnp.sum(total, axis=0, keepdims=True)], axis=0)

    def gather(order, j):
        return jnp.concatenate(
            [
                jnp.dot(
                    pbuf[order, (j * heads_each + e) * rows : (j * heads_each + e + 1) * rows, :],
                    vbuf[order * CHUNKS + j, :, e * HD : (e + 1) * HD], preferred_element_type=jnp.float32,
                )
                for e in range(heads_each)
            ],
            axis=0,
        )

    def remote(src, dst, ss, rs, device):
        return pltpu.make_async_remote_copy(
            src_ref=src, dst_ref=dst, send_sem=ss, recv_sem=rs, device_id={"seq": device}, device_id_type=MESH
        )

    def ml_to_partner():
        return remote(half_ml, peer_ml, hsm, hrm, partner)

    def num_to_partner(j):
        return remote(half_num.at[j], peer_num.at[j], hs.at[j], hr.at[j], partner)

    targets = [0, 1, middle * 2, middle * 2 + 1]

    def ml_to_root(i):
        return remote(chip_ml.at[chip], chip_ml.at[chip], csm.at[i], crm.at[chip], targets[i] * 2 + core)

    def num_to_root(j, i):
        return remote(chip_num.at[j, chip], chip_num.at[j, chip], cs.at[j, i], cr.at[j, chip], targets[i] * 2 + core)

    def ml_from_chip(k):
        slot = (chip + k) % chips
        return remote(chip_ml.at[slot], chip_ml.at[slot], csm.at[0], crm.at[slot], slot * 2 + core)

    def num_from_chip(j, k):
        slot = (chip + k) % chips
        return remote(chip_num.at[j, slot], chip_num.at[j, slot], cs.at[j, 0], cr.at[j, slot], slot * 2 + core)

    def part_of(owner, j):
        return out.at[:, pl.ds(pl.multiple_of(owner * (CHUNKS * span) + j * span, span), span), :]

    def elsewhere(i, act):
        @pl.when(chip != targets[i])
        def _():
            act()

    k_copy(0).wait()
    top = score(0, 0, None)
    k_copy(1).wait()
    top = score(0, 1, top)
    k_copy(2).wait()
    half_ml[...] = weigh(0, top)
    own_top = score(1, 0, None)
    @pl.when(first)
    def _():
        pl.semaphore_wait(barrier, 4)

    @pl.when(central)
    def _():
        pl.semaphore_wait(barrier, 5 + 4 * len(guests))

    @pl.when(guest)
    def _():
        pl.semaphore_wait(barrier, 5)

    ml_to_partner().start()
    for j in range(CHUNKS):
        v_copy(j).wait()
    for j in range(CHUNKS):
        half_num[j] = gather(0, j).astype(jnp.bfloat16)
    for j in range(CHUNKS):
        num_to_partner(j).start()
    k_copy(3).wait()
    own_top = score(1, 1, own_top)
    ml = weigh(1, own_top)
    ml_to_partner().wait_recv()
    other = peer_ml[...]
    top = jnp.maximum(ml[0:1], other[0:1])
    mine = jnp.exp2((ml[0:1] - top) * SHIFT)
    theirs = jnp.exp2((other[0:1] - top) * SHIFT)
    chip_ml[chip] = jnp.concatenate([top, mine * ml[1:2] + theirs * other[1:2]], axis=0)
    columns = jnp.transpose(jnp.concatenate([mine, theirs, jnp.zeros((6, lanes), jnp.float32)], axis=0))
    for i in range(len(targets)):
        elsewhere(i, lambda: ml_to_root(i).start())
    for j in range(CHUNKS):
        v_copy(CHUNKS + j).wait()
    numers = [gather(1, j) for j in range(CHUNKS)]
    for j in range(CHUNKS):
        num_to_partner(j).wait_recv()
        some = slice(j * block, (j + 1) * block)
        total = numers[j] * columns[some, 0:1] + peer_num[j].astype(jnp.float32) * columns[some, 1:2]
        chip_num[j, chip] = total.astype(jnp.bfloat16)
        elsewhere(0, lambda: num_to_root(j, 0).start())
    for j in range(CHUNKS):
        elsewhere(2 + j, lambda: num_to_root(j, 2 + j).start())
    @pl.when(core == 1)
    def _():
        for j in range(CHUNKS):
            elsewhere(0, lambda: num_to_root(j, 0).wait_send())

    for j in range(CHUNKS):
        elsewhere(1, lambda: num_to_root(j, 1).start())

    def share(j):
        yield (0, partner), remote(part_of(core, j), part_of(core, j), fs.at[0], fr.at[core, j], partner)
        for d in range(2):
            yield (1 + d, across + d), remote(part_of(core, j), part_of(core, j), fs.at[1 + d], fr.at[core, j], across + d)
        for g, p in enumerate(guests):
            for d in range(4):
                yield (3 + 4 * g + d, p * 4 + d), remote(
                    part_of(core, j), part_of(core, j), fs.at[3 + 4 * g + d], fr.at[core, j], p * 4 + d
                )

    def collect(j, columns):
        for k in range(1, chips):
            num_from_chip(j, k).wait_recv()
        numer = None
        for i in range(chips):
            term = chip_num[j, i].astype(jnp.float32) * columns[j * block : (j + 1) * block, i : i + 1]
            numer = term if numer is None else numer + term
        attended = numer.astype(jnp.bfloat16)
        for e in range(heads_each):
            for t in range(2):
                base = pl.multiple_of(core * (CHUNKS * span) + j * span + e * tile, tile)
                out[t, pl.ds(base, tile), :] = attended[e * rows + t * tile : e * rows + (t + 1) * tile]

    def factors_of_chips():
        for k in range(1, chips):
            ml_from_chip(k).wait_recv()
        maxima = [chip_ml[i][0:1] for i in range(chips)]
        top = functools.reduce(jnp.maximum, maxima)
        factors = [jnp.exp2((m - top) * SHIFT) for m in maxima]
        denom = sum(f * chip_ml[i][1:2] for i, f in enumerate(factors))
        factors = [f / denom for f in factors]
        pad = -chips % 8
        if pad:
            factors = factors + [jnp.zeros((pad, lanes), jnp.float32)]
        return jnp.transpose(jnp.concatenate(factors, axis=0))

    def swap(j, owner):
        return remote(part_of(core, j), part_of(owner, j), ps.at[j], pr.at[j], partner)

    @pl.when(first)
    def _():
        columns = factors_of_chips()
        for j in range(CHUNKS):
            collect(j, columns)
            swap(j, core).start()
        for j in range(CHUNKS):
            swap(j, 1 - core).wait_recv()
        for j in range(CHUNKS):
            swap(j, core).wait_send()

    for j in range(CHUNKS):
        @pl.when(central & (y == j))
        def _():
            collect(j, factors_of_chips())
            for _, copy in share(j):
                copy.start()

    @pl.when(jnp.logical_not(first))
    def _():
        for d in range(2):
            for j in range(CHUNKS):
                @pl.when(jnp.logical_not(central & (core == d) & (y == j)))
                def _():
                    remote(part_of(d, j), part_of(d, j), fs.at[0], fr.at[d, j], (middle * 2 + j) * 2 + d).wait_recv()

    for j in range(CHUNKS):
        @pl.when(central & (y == j))
        def _():
            for _, copy in share(j):
                copy.wait_send()

    ml_to_partner().wait_send()
    for j in range(CHUNKS):
        num_to_partner(j).wait_send()
        for i in (0, 1, 2 + j):
            @pl.when((core == 0) | (i != 0))
            def _():
                elsewhere(i, lambda: num_to_root(j, i).wait_send())
    for i in range(len(targets)):
        elsewhere(i, lambda: ml_to_root(i).wait_send())


def per_device(n, queries, cache_k, cache_v, context_len, slot_seq, slot_pos):
    slots = cache_k.shape[0]
    seqs = queries.shape[1]
    heads = queries.shape[2] // HD
    rows = 2 * seqs * heads // KVH
    heads_half = KVH // 2
    lanes = heads_half * rows
    block = lanes // CHUNKS
    chips = n // 2
    vmem = pl.BlockSpec(memory_space=pltpu.VMEM)
    dma = pltpu.SemaphoreType.DMA
    anywhere = pl.BlockSpec(memory_space=pltpu.HBM)
    attended = pl.pallas_call(
        functools.partial(kernel, n),
        out_shape=jax.ShapeDtypeStruct((2, heads * seqs, HD), jnp.bfloat16),
        in_specs=[anywhere] * 6,
        out_specs=vmem,
        scratch_shapes=[
            pltpu.SMEM((seqs,), jnp.int32),
            pltpu.VMEM(queries.shape, jnp.bfloat16),
            pltpu.VMEM((1, slots), jnp.int32),
            pltpu.VMEM((1, slots), jnp.int32),
            pltpu.VMEM((2, slots, heads_half * HD), jnp.bfloat16),
            pltpu.VMEM((2 * CHUNKS, slots, heads_half * HD // CHUNKS), jnp.bfloat16),
            pltpu.VMEM((KVH * rows, HD), jnp.float32),
            pltpu.VMEM((2, heads_half * HD, lanes), jnp.bfloat16),
            pltpu.VMEM((slots, lanes), jnp.float32),
            pltpu.VMEM((2, slots, lanes), jnp.float32),
            pltpu.VMEM((2, lanes, slots), jnp.bfloat16),
            pltpu.VMEM((CHUNKS, block, HD), jnp.bfloat16),
            pltpu.VMEM((2, lanes), jnp.float32),
            pltpu.VMEM((CHUNKS, block, HD), jnp.bfloat16),
            pltpu.VMEM((2, lanes), jnp.float32),
            pltpu.VMEM((CHUNKS, chips, block, HD), jnp.bfloat16),
            pltpu.VMEM((chips, 2, lanes), jnp.float32),
            dma((4,)), dma((2 * CHUNKS,)), dma((2 * CHUNKS,)),
            dma((CHUNKS,)), dma(()), dma((CHUNKS,)), dma(()),
            dma((CHUNKS, 4)), dma((4,)), dma((CHUNKS, chips)), dma((chips,)),
            dma((CHUNKS,)), dma((CHUNKS,)),
            dma((4 * chips,)), dma((2, CHUNKS)),
        ],
        compiler_params=pltpu.CompilerParams(collective_id=0, has_side_effects=True, vmem_limit_bytes=LIMIT),
    )(*[
        pltpu.with_memory_space_constraint(x, pltpu.HBM)
        for x in (context_len, queries, cache_k, cache_v, slot_seq.reshape(1, slots), slot_pos.reshape(1, slots))
    ])
    steps = queries.shape[0]
    return attended.reshape(steps, heads, seqs, HD).transpose(0, 2, 1, 3).reshape(queries.shape)


def solution(mesh):
    return jax.shard_map(
        functools.partial(per_device, mesh.shape["seq"]),
        mesh=mesh,
        in_specs=(
            P(None, "parts", None),
            P(("parts", "seq"), None),
            P(("parts", "seq"), None),
            P("parts"),
            P(("parts", "seq")),
            P(("parts", "seq")),
        ),
        out_specs=P(None, "parts", None),
        check_vma=False,
    )
```

```python
import functools

import jax
import jax.numpy as jnp
from jax import lax
from jax.experimental import pallas as pl
from jax.experimental.pallas import tpu as pltpu
from jax.sharding import PartitionSpec as P

KVH = 8
HD = 128
CHUNKS = 2
STEP = 256
LIMIT = 24 << 20
SHIFT = HD ** (-0.5) * 1.4426950408889634
HIDDEN = -1e30
MESH = pl.DeviceIdType.MESH


def kernel(
    n, ctx_hbm, q_hbm, k_hbm, v_hbm, seq_hbm, pos_hbm, out,
    ctx, q_ref, seq_ref, pos_ref, kbuf, vbuf, qf, qt, bias, sbuf, pbuf,
    half_num, half_ml, peer_num, peer_ml, chip_num, chip_ml,
    isem, ksem, vsem, peer_sem, ml_sem, num_sem, fin,
):
    me = lax.axis_index("seq")
    chips = n // 2
    planes = chips // 2
    core = me % 2
    chip = me // 2
    y = chip % 2
    plane = chip // 2
    middle = planes // 2
    first, central = plane == 0, plane == middle
    guests = [p for p in range(planes) if p not in (0, middle)]
    guest = jnp.logical_not(first | central)
    partner = chip * 2 + (1 - core)
    across = (plane * 2 + (1 - y)) * 2
    halves = (1 - core, core)
    slots = k_hbm.shape[0]
    heads_half = KVH // 2
    heads_each = heads_half // CHUNKS
    wide = heads_half * HD
    width = heads_each * HD
    group = q_ref.shape[2] // HD // KVH
    seqs = q_ref.shape[1]
    rows = 2 * seqs * group
    lanes = heads_half * rows
    block = heads_each * rows
    tile = group * seqs
    span = heads_each * tile
    cut = slots // CHUNKS

    barrier = pltpu.get_barrier_semaphore()

    def greet(device):
        pl.semaphore_signal(barrier, inc=1, device_id={"seq": device}, device_id_type=MESH)

    inputs = []
    for i, (src, dst) in enumerate(((q_hbm, q_ref), (seq_hbm, seq_ref), (pos_hbm, pos_ref), (ctx_hbm, ctx))):
        copy = pltpu.make_async_copy(src, dst, isem.at[i])
        copy.start()
        inputs.append(copy)

    def first_column(order):
        half = core * order + (1 - core) * (1 - order)
        return half * wide

    def k_copy(i):
        order, part = i // CHUNKS, i % CHUNKS
        some = pl.ds(pl.multiple_of(part * cut, cut), cut)
        columns = pl.ds(pl.multiple_of(first_column(order), wide), wide)
        return pltpu.make_async_copy(k_hbm.at[some, columns], kbuf.at[order, some], ksem.at[i])

    def v_copy(i):
        order, part = i // CHUNKS, i % CHUNKS
        columns = pl.ds(pl.multiple_of(first_column(order) + part * width, width), width)
        return pltpu.make_async_copy(v_hbm.at[:, columns], vbuf.at[i], vsem.at[order])

    def load_k(i, carry):
        k_copy(i).start()
        return carry

    def load_v(i, carry):
        v_copy(i).start()
        return carry

    lax.fori_loop(0, 3, load_k, 0)
    lax.fori_loop(0, 2, load_v, 0)
    k_copy(3).start()
    lax.fori_loop(2, 4, load_v, 0)

    greet(partner)

    @pl.when(first | central)
    def _():
        for k in range(1, chips):
            greet((chip + k) % chips * 2 + core)

    @pl.when(central)
    def _():
        greet(across + (1 - core))

    @pl.when(guest)
    def _():
        for d in range(4):
            greet(middle * 4 + d)

    for copy in inputs:
        copy.wait()

    for t in range(2):
        for head in range(KVH * group):
            g, h = head // group, head % group
            base = g * rows + t * group * seqs + h * seqs
            qf[base : base + seqs, :] = q_ref[t, :, head * HD : (head + 1) * HD].astype(jnp.float32)

    column = lax.broadcasted_iota(jnp.int32, (HD, lanes), 1)
    for order in range(2):
        turned = jnp.transpose(qf[pl.ds(pl.multiple_of(halves[order] * lanes, lanes), lanes), :])
        for e in range(heads_half):
            qt[order, e * HD : (e + 1) * HD, :] = jnp.where(column // rows == e, turned, 0.0).astype(jnp.bfloat16)

    masks = []
    for t in range(2):
        for sq in range(seqs):
            allowed = (seq_ref[...] == sq) & (pos_ref[...] <= ctx[sq] - 2 + t)
            masks.append(jnp.where(allowed, 0.0, HIDDEN))
    pad = -len(masks) % 16
    masks = jnp.concatenate(masks + [jnp.zeros((pad, slots), jnp.float32)], axis=0).astype(jnp.bfloat16)
    pick_row = lax.broadcasted_iota(jnp.int32, (2 * seqs + pad, lanes), 0)
    pick_lane = lax.broadcasted_iota(jnp.int32, (2 * seqs + pad, lanes), 1) % rows
    pick = (pick_lane // tile) * seqs + pick_lane % seqs == pick_row
    bias[...] = lax.dot_general(
        masks, jnp.where(pick, 1.0, 0.0).astype(jnp.bfloat16), (((0,), (0,)), ((), ())),
        preferred_element_type=jnp.float32,
    )

    def fold(x, op):
        return op(x.reshape(x.shape[0] // 8, 8, x.shape[1]), axis=0)

    def score(order, part, top):
        for b in range(part * cut, (part + 1) * cut, STEP):
            got = jnp.dot(
                kbuf[order, b : b + STEP, :], qt[order], preferred_element_type=jnp.float32
            ) + bias[b : b + STEP, :]
            sbuf[order, b : b + STEP, :] = got
            high = fold(got, jnp.max)
            top = high if top is None else jnp.maximum(top, high)
        return top

    def weigh(order, top):
        m = jnp.max(top, axis=0, keepdims=True)
        total = None
        for b in range(0, slots, STEP):
            w = jnp.exp2((sbuf[order, b : b + STEP, :] - m) * SHIFT)
            pbuf[order, :, b : b + STEP] = jnp.transpose(w.astype(jnp.bfloat16))
            part = fold(w, jnp.sum)
            total = part if total is None else total + part
        return jnp.concatenate([m, jnp.sum(total, axis=0, keepdims=True)], axis=0)

    def gather(order, j):
        return jnp.concatenate(
            [
                jnp.dot(
                    pbuf[order, (j * heads_each + e) * rows : (j * heads_each + e + 1) * rows, :],
                    vbuf[order * CHUNKS + j, :, e * HD : (e + 1) * HD], preferred_element_type=jnp.float32,
                )
                for e in range(heads_each)
            ],
            axis=0,
        )

    def drain(ref, sem):
        pltpu.make_async_copy(ref, ref, sem).wait()

    rest_sent, ml_sent, first_sent, shared = (isem.at[i] for i in range(4))

    def remote(src, dst, ss, rs, device):
        return pltpu.make_async_remote_copy(
            src_ref=src, dst_ref=dst, send_sem=ss, recv_sem=rs, device_id={"seq": device}, device_id_type=MESH
        )

    def ml_to_partner():
        return remote(half_ml, peer_ml, ml_sent, peer_sem.at[0], partner)

    def num_to_partner(j):
        return remote(half_num.at[j], peer_num.at[j], rest_sent, peer_sem.at[1], partner)

    targets = [0, 1, middle * 2, middle * 2 + 1]

    def ml_to_root(i):
        return remote(chip_ml.at[chip], chip_ml.at[chip], ml_sent, ml_sem, targets[i] * 2 + core)

    def num_to_root(j, i):
        sent = rest_sent if i else first_sent
        return remote(chip_num.at[j, chip], chip_num.at[j, chip], sent, num_sem.at[j], targets[i] * 2 + core)

    def part_of(owner, j):
        return out.at[:, pl.ds(pl.multiple_of(owner * (CHUNKS * span) + j * span, span), span), :]

    def elsewhere(i, act):
        @pl.when(chip != targets[i])
        def _():
            act()

    k_copy(0).wait()
    top = score(0, 0, None)
    k_copy(1).wait()
    top = score(0, 1, top)
    k_copy(2).wait()
    half_ml[...] = weigh(0, top)
    own_top = score(1, 0, None)
    @pl.when(first)
    def _():
        pl.semaphore_wait(barrier, 4)

    @pl.when(central)
    def _():
        pl.semaphore_wait(barrier, 5 + 4 * len(guests))

    @pl.when(guest)
    def _():
        pl.semaphore_wait(barrier, 5)

    ml_to_partner().start()
    drain(vbuf.at[:CHUNKS], vsem.at[0])
    for j in range(CHUNKS):
        half_num[j] = gather(0, j).astype(jnp.bfloat16)
    for j in range(CHUNKS):
        num_to_partner(j).start()
    k_copy(3).wait()
    own_top = score(1, 1, own_top)
    ml = weigh(1, own_top)
    drain(peer_ml, peer_sem.at[0])
    other = peer_ml[...]
    top = jnp.maximum(ml[0:1], other[0:1])
    mine = jnp.exp2((ml[0:1] - top) * SHIFT)
    theirs = jnp.exp2((other[0:1] - top) * SHIFT)
    chip_ml[chip] = jnp.concatenate([top, mine * ml[1:2] + theirs * other[1:2]], axis=0)
    columns = jnp.transpose(jnp.concatenate([mine, theirs, jnp.zeros((6, lanes), jnp.float32)], axis=0))
    for i in range(len(targets)):
        elsewhere(i, lambda: ml_to_root(i).start())
    drain(vbuf.at[CHUNKS:], vsem.at[1])
    numers = [gather(1, j) for j in range(CHUNKS)]
    drain(peer_num, peer_sem.at[1])
    for j in range(CHUNKS):
        some = slice(j * block, (j + 1) * block)
        total = numers[j] * columns[some, 0:1] + peer_num[j].astype(jnp.float32) * columns[some, 1:2]
        chip_num[j, chip] = total.astype(jnp.bfloat16)
        elsewhere(0, lambda: num_to_root(j, 0).start())
    @pl.when(core == 1)
    def _():
        elsewhere(0, lambda: drain(chip_num.at[0, :CHUNKS], first_sent))

    for j in range(CHUNKS):
        elsewhere(2 + j, lambda: num_to_root(j, 2 + j).start())
    for j in range(CHUNKS):
        elsewhere(1, lambda: num_to_root(j, 1).start())

    def share(j):
        fans = [partner, across, across + 1] + [p * 4 + d for p in guests for d in range(4)]
        return [remote(part_of(core, j), part_of(core, j), shared, fin, device) for device in fans]

    def collect(j, columns):
        drain(chip_num.at[j, : chips - 1], num_sem.at[j])
        numer = None
        for i in range(chips):
            term = chip_num[j, i].astype(jnp.float32) * columns[j * block : (j + 1) * block, i : i + 1]
            numer = term if numer is None else numer + term
        attended = numer.astype(jnp.bfloat16)
        for e in range(heads_each):
            for t in range(2):
                base = pl.multiple_of(core * (CHUNKS * span) + j * span + e * tile, tile)
                out[t, pl.ds(base, tile), :] = attended[e * rows + t * tile : e * rows + (t + 1) * tile]

    def factors_of_chips():
        drain(chip_ml.at[: chips - 1], ml_sem)
        maxima = [chip_ml[i][0:1] for i in range(chips)]
        top = functools.reduce(jnp.maximum, maxima)
        factors = [jnp.exp2((m - top) * SHIFT) for m in maxima]
        denom = sum(f * chip_ml[i][1:2] for i, f in enumerate(factors))
        factors = [f / denom for f in factors]
        pad = -chips % 8
        if pad:
            factors = factors + [jnp.zeros((pad, lanes), jnp.float32)]
        return jnp.transpose(jnp.concatenate(factors, axis=0))

    @pl.when(first)
    def _():
        columns = factors_of_chips()
        for j in range(CHUNKS):
            collect(j, columns)
            remote(part_of(core, j), part_of(core, j), shared, fin, partner).start()

    for j in range(CHUNKS):
        @pl.when(central & (y == j))
        def _():
            collect(j, factors_of_chips())
            for copy in share(j):
                copy.start()

    def sent(units, sem):
        drain(kbuf.at[0, : units * block * HD // wide], sem)

    for who, at_roots, others in (
        (guest, 4, 6), (central, 3, 5), (chip == 0, 3, 6), (chip == 1, 3, 4),
    ):
        @pl.when(who)
        def _():
            drain(chip_ml.at[: 1 + at_roots], ml_sent)
            sent(others, rest_sent)

    @pl.when(core == 0)
    def _():
        elsewhere(0, lambda: drain(chip_num.at[0, :CHUNKS], first_sent))

    @pl.when(first)
    def _():
        drain(out.at[:, : CHUNKS * span], fin)
        sent(CHUNKS, shared)

    @pl.when(central)
    def _():
        drain(out.at[:, : 3 * span], fin)
        sent(3 + 4 * len(guests), shared)

    @pl.when(guest)
    def _():
        drain(out, fin)


def per_device(n, queries, cache_k, cache_v, context_len, slot_seq, slot_pos):
    slots = cache_k.shape[0]
    seqs = queries.shape[1]
    heads = queries.shape[2] // HD
    rows = 2 * seqs * heads // KVH
    heads_half = KVH // 2
    lanes = heads_half * rows
    block = lanes // CHUNKS
    chips = n // 2
    vmem = pl.BlockSpec(memory_space=pltpu.VMEM)
    dma = pltpu.SemaphoreType.DMA
    anywhere = pl.BlockSpec(memory_space=pltpu.HBM)
    attended = pl.pallas_call(
        functools.partial(kernel, n),
        out_shape=jax.ShapeDtypeStruct((2, heads * seqs, HD), jnp.bfloat16),
        in_specs=[anywhere] * 6,
        out_specs=vmem,
        scratch_shapes=[
            pltpu.SMEM((seqs,), jnp.int32),
            pltpu.VMEM(queries.shape, jnp.bfloat16),
            pltpu.VMEM((1, slots), jnp.int32),
            pltpu.VMEM((1, slots), jnp.int32),
            pltpu.VMEM((2, slots, heads_half * HD), jnp.bfloat16),
            pltpu.VMEM((2 * CHUNKS, slots, heads_half * HD // CHUNKS), jnp.bfloat16),
            pltpu.VMEM((KVH * rows, HD), jnp.float32),
            pltpu.VMEM((2, heads_half * HD, lanes), jnp.bfloat16),
            pltpu.VMEM((slots, lanes), jnp.float32),
            pltpu.VMEM((2, slots, lanes), jnp.float32),
            pltpu.VMEM((2, lanes, slots), jnp.bfloat16),
            pltpu.VMEM((CHUNKS, block, HD), jnp.bfloat16),
            pltpu.VMEM((2, lanes), jnp.float32),
            pltpu.VMEM((CHUNKS, block, HD), jnp.bfloat16),
            pltpu.VMEM((2, lanes), jnp.float32),
            pltpu.VMEM((CHUNKS, chips, block, HD), jnp.bfloat16),
            pltpu.VMEM((chips, 2, lanes), jnp.float32),
            dma((4,)), dma((2 * CHUNKS,)), dma((2,)), dma((2,)), dma(()), dma((CHUNKS,)), dma(()),
        ],
        compiler_params=pltpu.CompilerParams(collective_id=0, has_side_effects=True, vmem_limit_bytes=LIMIT),
    )(*[
        pltpu.with_memory_space_constraint(x, pltpu.HBM)
        for x in (context_len, queries, cache_k, cache_v, slot_seq.reshape(1, slots), slot_pos.reshape(1, slots))
    ])
    steps = queries.shape[0]
    return attended.reshape(steps, heads, seqs, HD).transpose(0, 2, 1, 3).reshape(queries.shape)


def solution(mesh):
    return jax.shard_map(
        functools.partial(per_device, mesh.shape["seq"]),
        mesh=mesh,
        in_specs=(
            P(None, "parts", None),
            P(("parts", "seq"), None),
            P(("parts", "seq"), None),
            P("parts"),
            P(("parts", "seq")),
            P(("parts", "seq")),
        ),
        out_specs=P(None, "parts", None),
        check_vma=False,
    )
```

```python
import functools

import jax
import jax.numpy as jnp
from jax import lax
from jax.experimental import pallas as pl
from jax.experimental.pallas import tpu as pltpu
from jax.sharding import PartitionSpec as P

KVH = 8
HD = 128
CHUNKS = 2
STEP = 256
LIMIT = 24 << 20
SHIFT = HD ** (-0.5) * 1.4426950408889634
HIDDEN = -1e30
MESH = pl.DeviceIdType.MESH


def kernel(
    n, ctx_hbm, q_hbm, k_hbm, v_hbm, seq_hbm, pos_hbm, out,
    ctx, q_ref, seq_ref, pos_ref, kbuf, vbuf, qf, qt, bias, sbuf, pbuf,
    half_num, half_ml, peer_num, peer_ml, chip_num, chip_ml,
    isem, ksem, vsem, peer_sem, ml_sem, num_sem, fin,
):
    me = lax.axis_index("seq")
    chips = n // 2
    planes = chips // 2
    core = me % 2
    chip = me // 2
    y = chip % 2
    plane = chip // 2
    middle = planes // 2
    first, central = plane == 0, plane == middle
    guests = [p for p in range(planes) if p not in (0, middle)]
    guest = jnp.logical_not(first | central)
    partner = chip * 2 + (1 - core)
    across = (plane * 2 + (1 - y)) * 2
    halves = (1 - core, core)
    slots = k_hbm.shape[0]
    heads_half = KVH // 2
    heads_each = heads_half // CHUNKS
    wide = heads_half * HD
    width = heads_each * HD
    group = q_ref.shape[2] // HD // KVH
    seqs = q_ref.shape[1]
    rows = 2 * seqs * group
    lanes = heads_half * rows
    block = heads_each * rows
    tile = group * seqs
    span = heads_each * tile
    cut = slots // CHUNKS

    barrier = pltpu.get_barrier_semaphore()

    def greet(device):
        pl.semaphore_signal(barrier, inc=1, device_id={"seq": device}, device_id_type=MESH)

    inputs = []
    for i, (src, dst) in enumerate(((q_hbm, q_ref), (seq_hbm, seq_ref), (pos_hbm, pos_ref), (ctx_hbm, ctx))):
        copy = pltpu.make_async_copy(src, dst, isem.at[i])
        copy.start()
        inputs.append(copy)

    def first_column(order):
        half = core * order + (1 - core) * (1 - order)
        return half * wide

    def k_copy(i):
        order, part = i // CHUNKS, i % CHUNKS
        some = pl.ds(pl.multiple_of(part * cut, cut), cut)
        columns = pl.ds(pl.multiple_of(first_column(order), wide), wide)
        return pltpu.make_async_copy(k_hbm.at[some, columns], kbuf.at[order, some], ksem.at[i])

    def v_copy(order):
        columns = pl.ds(pl.multiple_of(first_column(order), wide), wide)
        return pltpu.make_async_copy(v_hbm.at[:, columns], vbuf.at[order], vsem.at[order])

    def load_k(i, carry):
        k_copy(i).start()
        return carry

    def load_v(order, carry):
        v_copy(order).start()

        @pl.when(order == 0)
        def _():
            k_copy(2 * CHUNKS - 1).start()

        return carry

    lax.fori_loop(0, 2 * CHUNKS - 1, load_k, 0)
    lax.fori_loop(0, 2, load_v, 0)

    greet(partner)

    @pl.when(first | central)
    def _():
        for k in range(1, chips):
            greet((chip + k) % chips * 2 + core)

    @pl.when(central)
    def _():
        greet(across + (1 - core))

    @pl.when(guest)
    def _():
        for d in range(4):
            greet(middle * 4 + d)

    for copy in inputs:
        copy.wait()

    for t in range(2):
        for head in range(KVH * group):
            g, h = head // group, head % group
            base = g * rows + t * group * seqs + h * seqs
            qf[base : base + seqs, :] = q_ref[t, :, head * HD : (head + 1) * HD].astype(jnp.float32)

    column = lax.broadcasted_iota(jnp.int32, (HD, lanes), 1)
    for order in range(2):
        turned = jnp.transpose(qf[pl.ds(pl.multiple_of(halves[order] * lanes, lanes), lanes), :])
        for e in range(heads_half):
            qt[order, e * HD : (e + 1) * HD, :] = jnp.where(column // rows == e, turned, 0.0).astype(jnp.bfloat16)

    masks = []
    for t in range(2):
        for sq in range(seqs):
            allowed = (seq_ref[...] == sq) & (pos_ref[...] <= ctx[sq] - 2 + t)
            masks.append(jnp.where(allowed, 0.0, HIDDEN))
    pad = -len(masks) % 16
    masks = jnp.concatenate(masks + [jnp.zeros((pad, slots), jnp.float32)], axis=0).astype(jnp.bfloat16)
    pick_row = lax.broadcasted_iota(jnp.int32, (2 * seqs + pad, lanes), 0)
    pick_lane = lax.broadcasted_iota(jnp.int32, (2 * seqs + pad, lanes), 1) % rows
    pick = (pick_lane // tile) * seqs + pick_lane % seqs == pick_row
    bias[...] = lax.dot_general(
        masks, jnp.where(pick, 1.0, 0.0).astype(jnp.bfloat16), (((0,), (0,)), ((), ())),
        preferred_element_type=jnp.float32,
    )

    def fold(x, op):
        return op(x.reshape(x.shape[0] // 8, 8, x.shape[1]), axis=0)

    def score(order, part, top):
        for b in range(part * cut, (part + 1) * cut, STEP):
            got = jnp.dot(
                kbuf[order, b : b + STEP, :], qt[order], preferred_element_type=jnp.float32
            ) + bias[b : b + STEP, :]
            sbuf[order, b : b + STEP, :] = got
            high = fold(got, jnp.max)
            top = high if top is None else jnp.maximum(top, high)
        return top

    def weigh(order, top):
        m = jnp.max(top, axis=0, keepdims=True)
        total = None
        for b in range(0, slots, STEP):
            w = jnp.exp2((sbuf[order, b : b + STEP, :] - m) * SHIFT)
            pbuf[order, :, b : b + STEP] = jnp.transpose(w.astype(jnp.bfloat16))
            part = fold(w, jnp.sum)
            total = part if total is None else total + part
        return jnp.concatenate([m, jnp.sum(total, axis=0, keepdims=True)], axis=0)

    def gather(order, j):
        return jnp.concatenate(
            [
                jnp.dot(
                    pbuf[order, (j * heads_each + e) * rows : (j * heads_each + e + 1) * rows, :],
                    vbuf[order, :, j * width + e * HD : j * width + (e + 1) * HD], preferred_element_type=jnp.float32,
                )
                for e in range(heads_each)
            ],
            axis=0,
        )

    def drain(ref, sem):
        pltpu.make_async_copy(ref, ref, sem).wait()

    rest_sent, ml_sent, first_sent, shared = (isem.at[i] for i in range(4))

    def remote(src, dst, ss, rs, device):
        return pltpu.make_async_remote_copy(
            src_ref=src, dst_ref=dst, send_sem=ss, recv_sem=rs, device_id={"seq": device}, device_id_type=MESH
        )

    def ml_to_partner():
        return remote(half_ml, peer_ml, ml_sent, peer_sem.at[0], partner)

    def num_to_partner(j):
        return remote(half_num.at[j], peer_num.at[j], rest_sent, peer_sem.at[1], partner)

    targets = [0, 1, middle * 2, middle * 2 + 1]
    late = plane // (planes - 1)

    def ml_to_root(i):
        return remote(chip_ml.at[chip], chip_ml.at[chip], ml_sent, ml_sem, targets[i] * 2 + core)

    def num_to_root(j, i):
        sent = rest_sent if i else first_sent
        return remote(chip_num.at[j, chip], chip_num.at[j, chip], sent, num_sem.at[late * CHUNKS + j], targets[i] * 2 + core)

    def part_of(owner, j):
        return out.at[:, pl.ds(pl.multiple_of(owner * (CHUNKS * span) + j * span, span), span), :]

    def elsewhere(i, act):
        @pl.when(chip != targets[i])
        def _():
            act()

    k_copy(0).wait()
    top = score(0, 0, None)
    k_copy(1).wait()
    top = score(0, 1, top)
    k_copy(2).wait()
    half_ml[...] = weigh(0, top)
    own_top = score(1, 0, None)
    @pl.when(first)
    def _():
        pl.semaphore_wait(barrier, 4)

    @pl.when(central)
    def _():
        pl.semaphore_wait(barrier, 5 + 4 * len(guests))

    @pl.when(guest)
    def _():
        pl.semaphore_wait(barrier, 5)

    ml_to_partner().start()
    v_copy(0).wait()
    for j in range(CHUNKS):
        half_num[j] = gather(0, j).astype(jnp.bfloat16)
    for j in range(CHUNKS):
        num_to_partner(j).start()
    k_copy(3).wait()
    own_top = score(1, 1, own_top)
    ml = weigh(1, own_top)
    drain(peer_ml, peer_sem.at[0])
    other = peer_ml[...]
    top = jnp.maximum(ml[0:1], other[0:1])
    mine = jnp.exp2((ml[0:1] - top) * SHIFT)
    theirs = jnp.exp2((other[0:1] - top) * SHIFT)
    chip_ml[chip] = jnp.concatenate([top, mine * ml[1:2] + theirs * other[1:2]], axis=0)
    columns = jnp.transpose(jnp.concatenate([mine, theirs, jnp.zeros((6, lanes), jnp.float32)], axis=0))
    for i in range(len(targets)):
        elsewhere(i, lambda: ml_to_root(i).start())
    v_copy(1).wait()
    numers = [gather(1, j) for j in range(CHUNKS)]
    drain(peer_num, peer_sem.at[1])
    for j in range(CHUNKS):
        some = slice(j * block, (j + 1) * block)
        total = numers[j] * columns[some, 0:1] + peer_num[j].astype(jnp.float32) * columns[some, 1:2]
        chip_num[j, chip] = total.astype(jnp.bfloat16)
        elsewhere(0, lambda: num_to_root(j, 0).start())
    @pl.when(core == 1)
    def _():
        elsewhere(0, lambda: drain(chip_num.at[0, :CHUNKS], first_sent))

    for j in range(CHUNKS):
        elsewhere(2 + j, lambda: num_to_root(j, 2 + j).start())
    for j in range(CHUNKS):
        elsewhere(1, lambda: num_to_root(j, 1).start())

    def share(j):
        fans = [partner, across, across + 1] + [p * 4 + d for p in guests for d in range(4)]
        return [remote(part_of(core, j), part_of(core, j), shared, fin, device) for device in fans]

    def add_up(j, columns, some, numer):
        for i in some:
            term = chip_num[j, i].astype(jnp.float32) * columns[j * block : (j + 1) * block, i : i + 1]
            numer = term if numer is None else numer + term
        return numer

    def gather_early(j, columns):
        drain(chip_num.at[j, : chips - 3], num_sem.at[j])
        return add_up(j, columns, range(chips - 2), None)

    def collect(j, columns, numer):
        drain(chip_num.at[j, :2], num_sem.at[CHUNKS + j])
        attended = add_up(j, columns, range(chips - 2, chips), numer).astype(jnp.bfloat16)
        for e in range(heads_each):
            for t in range(2):
                base = pl.multiple_of(core * (CHUNKS * span) + j * span + e * tile, tile)
                out[t, pl.ds(base, tile), :] = attended[e * rows + t * tile : e * rows + (t + 1) * tile]

    def factors_of_chips():
        drain(chip_ml.at[: chips - 1], ml_sem)
        maxima = [chip_ml[i][0:1] for i in range(chips)]
        top = functools.reduce(jnp.maximum, maxima)
        factors = [jnp.exp2((m - top) * SHIFT) for m in maxima]
        denom = sum(f * chip_ml[i][1:2] for i, f in enumerate(factors))
        factors = [f / denom for f in factors]
        pad = -chips % 8
        if pad:
            factors = factors + [jnp.zeros((pad, lanes), jnp.float32)]
        return jnp.transpose(jnp.concatenate(factors, axis=0))

    @pl.when(first)
    def _():
        columns = factors_of_chips()
        early = [gather_early(j, columns) for j in range(CHUNKS)]
        for j in range(CHUNKS):
            collect(j, columns, early[j])
            remote(part_of(core, j), part_of(core, j), shared, fin, partner).start()

    for j in range(CHUNKS):
        @pl.when(central & (y == j))
        def _():
            columns = factors_of_chips()
            collect(j, columns, gather_early(j, columns))
            for copy in share(j):
                copy.start()

    def sent(units, sem):
        drain(kbuf.at[0, : units * block * HD // wide], sem)

    for who, at_roots, others in (
        (guest, 4, 6), (central, 3, 5), (chip == 0, 3, 6), (chip == 1, 3, 4),
    ):
        @pl.when(who)
        def _():
            drain(chip_ml.at[: 1 + at_roots], ml_sent)
            sent(others, rest_sent)

    @pl.when(core == 0)
    def _():
        elsewhere(0, lambda: drain(chip_num.at[0, :CHUNKS], first_sent))

    @pl.when(first)
    def _():
        drain(out.at[:, : CHUNKS * span], fin)
        sent(CHUNKS, shared)

    @pl.when(central)
    def _():
        drain(out.at[:, : 3 * span], fin)
        sent(3 + 4 * len(guests), shared)

    @pl.when(guest)
    def _():
        drain(out, fin)


def per_device(n, queries, cache_k, cache_v, context_len, slot_seq, slot_pos):
    slots = cache_k.shape[0]
    seqs = queries.shape[1]
    heads = queries.shape[2] // HD
    rows = 2 * seqs * heads // KVH
    heads_half = KVH // 2
    lanes = heads_half * rows
    block = lanes // CHUNKS
    chips = n // 2
    vmem = pl.BlockSpec(memory_space=pltpu.VMEM)
    dma = pltpu.SemaphoreType.DMA
    anywhere = pl.BlockSpec(memory_space=pltpu.HBM)
    attended = pl.pallas_call(
        functools.partial(kernel, n),
        out_shape=jax.ShapeDtypeStruct((2, heads * seqs, HD), jnp.bfloat16),
        in_specs=[anywhere] * 6,
        out_specs=vmem,
        scratch_shapes=[
            pltpu.SMEM((seqs,), jnp.int32),
            pltpu.VMEM(queries.shape, jnp.bfloat16),
            pltpu.VMEM((1, slots), jnp.int32),
            pltpu.VMEM((1, slots), jnp.int32),
            pltpu.VMEM((2, slots, heads_half * HD), jnp.bfloat16),
            pltpu.VMEM((2, slots, heads_half * HD), jnp.bfloat16),
            pltpu.VMEM((KVH * rows, HD), jnp.float32),
            pltpu.VMEM((2, heads_half * HD, lanes), jnp.bfloat16),
            pltpu.VMEM((slots, lanes), jnp.float32),
            pltpu.VMEM((2, slots, lanes), jnp.float32),
            pltpu.VMEM((2, lanes, slots), jnp.bfloat16),
            pltpu.VMEM((CHUNKS, block, HD), jnp.bfloat16),
            pltpu.VMEM((2, lanes), jnp.float32),
            pltpu.VMEM((CHUNKS, block, HD), jnp.bfloat16),
            pltpu.VMEM((2, lanes), jnp.float32),
            pltpu.VMEM((CHUNKS, chips, block, HD), jnp.bfloat16),
            pltpu.VMEM((chips, 2, lanes), jnp.float32),
            dma((4,)), dma((2 * CHUNKS,)), dma((2,)), dma((2,)), dma(()), dma((2 * CHUNKS,)), dma(()),
        ],
        compiler_params=pltpu.CompilerParams(collective_id=0, has_side_effects=True, vmem_limit_bytes=LIMIT),
    )(*[
        pltpu.with_memory_space_constraint(x, pltpu.HBM)
        for x in (context_len, queries, cache_k, cache_v, slot_seq.reshape(1, slots), slot_pos.reshape(1, slots))
    ])
    steps = queries.shape[0]
    return attended.reshape(steps, heads, seqs, HD).transpose(0, 2, 1, 3).reshape(queries.shape)


def solution(mesh):
    return jax.shard_map(
        functools.partial(per_device, mesh.shape["seq"]),
        mesh=mesh,
        in_specs=(
            P(None, "parts", None),
            P(("parts", "seq"), None),
            P(("parts", "seq"), None),
            P("parts"),
            P(("parts", "seq")),
            P(("parts", "seq")),
        ),
        out_specs=P(None, "parts", None),
        check_vma=False,
    )
```

```python
import functools

import jax
import jax.numpy as jnp
from jax import lax
from jax.experimental import pallas as pl
from jax.experimental.pallas import tpu as pltpu
from jax.sharding import PartitionSpec as P

KVH = 8
HD = 128
CHUNKS = 2
STEP = 256
LIMIT = 24 << 20
SHIFT = HD ** (-0.5) * 1.4426950408889634
HIDDEN = -1e30
MESH = pl.DeviceIdType.MESH


def kernel(
    n, ctx_hbm, q_hbm, k_hbm, v_hbm, seq_hbm, pos_hbm, out,
    ctx, q_ref, slot_ref, kbuf, vbuf, qf, qt, bias, sbuf, pbuf,
    half_num, half_ml, peer_num, peer_ml, chip_num, chip_ml,
    isem, ksem, vsem, peer_sem, ml_sem, num_sem, fin,
):
    me = lax.axis_index("seq")
    chips = n // 2
    planes = chips // 2
    core = me % 2
    chip = me // 2
    y = chip % 2
    plane = chip // 2
    middle = planes // 2
    first, central = plane == 0, plane == middle
    guests = [p for p in range(planes) if p not in (0, middle)]
    guest = jnp.logical_not(first | central)
    partner = chip * 2 + (1 - core)
    across = (plane * 2 + (1 - y)) * 2
    halves = (1 - core, core)
    slots = k_hbm.shape[0]
    heads_half = KVH // 2
    heads_each = heads_half // CHUNKS
    wide = heads_half * HD
    width = heads_each * HD
    group = q_ref.shape[2] // HD // KVH
    seqs = q_ref.shape[1]
    rows = 2 * seqs * group
    lanes = heads_half * rows
    block = heads_each * rows
    tile = group * seqs
    span = heads_each * tile
    cut = slots // CHUNKS

    barrier = pltpu.get_barrier_semaphore()

    def greet(device):
        pl.semaphore_signal(barrier, inc=1, device_id={"seq": device}, device_id_type=MESH)

    seq_ref, pos_ref = slot_ref.at[0], slot_ref.at[1]
    inputs = []
    for i, src, dst in ((0, q_hbm, q_ref), (1, seq_hbm, seq_ref), (1, pos_hbm, pos_ref), (2, ctx_hbm, ctx)):
        copy = pltpu.make_async_copy(src, dst, isem.at[i])
        copy.start()
        inputs.append(copy)

    def first_column(order):
        half = core * order + (1 - core) * (1 - order)
        return half * wide

    def k_copy(i):
        order, part = i // CHUNKS, i % CHUNKS
        some = pl.ds(pl.multiple_of(part * cut, cut), cut)
        columns = pl.ds(pl.multiple_of(first_column(order), wide), wide)
        return pltpu.make_async_copy(k_hbm.at[some, columns], kbuf.at[order, some], ksem.at[i])

    def v_copy(order):
        columns = pl.ds(pl.multiple_of(first_column(order), wide), wide)
        return pltpu.make_async_copy(v_hbm.at[:, columns], vbuf.at[order], vsem.at[order])

    def load_k(i, carry):
        k_copy(i).start()
        return carry

    def load_v(order, carry):
        v_copy(order).start()

        @pl.when(order == 0)
        def _():
            k_copy(2 * CHUNKS - 1).start()

        return carry

    lax.fori_loop(0, 2 * CHUNKS - 1, load_k, 0)
    lax.fori_loop(0, 2, load_v, 0)

    greet(partner)

    @pl.when(first | central)
    def _():
        for k in range(1, chips):
            greet((chip + k) % chips * 2 + core)

    @pl.when(central)
    def _():
        greet(across + (1 - core))

    @pl.when(guest)
    def _():
        for d in range(4):
            greet(middle * 4 + d)

    inputs[0].wait()
    pltpu.make_async_copy(slot_ref, slot_ref, isem.at[1]).wait()
    inputs[3].wait()

    for t in range(2):
        for head in range(KVH * group):
            g, h = head // group, head % group
            base = g * rows + t * group * seqs + h * seqs
            qf[base : base + seqs, :] = q_ref[t, :, head * HD : (head + 1) * HD].astype(jnp.float32)

    column = lax.broadcasted_iota(jnp.int32, (HD, lanes), 1)
    for order in range(2):
        turned = jnp.transpose(qf[pl.ds(pl.multiple_of(halves[order] * lanes, lanes), lanes), :])
        for e in range(heads_half):
            qt[order, e * HD : (e + 1) * HD, :] = jnp.where(column // rows == e, turned, 0.0).astype(jnp.bfloat16)

    masks = []
    for t in range(2):
        for sq in range(seqs):
            allowed = (seq_ref[...] == sq) & (pos_ref[...] <= ctx[sq] - 2 + t)
            masks.append(jnp.where(allowed, 0.0, HIDDEN))
    pad = -len(masks) % 16
    masks = jnp.concatenate(masks + [jnp.zeros((pad, slots), jnp.float32)], axis=0).astype(jnp.bfloat16)
    pick_row = lax.broadcasted_iota(jnp.int32, (2 * seqs + pad, lanes), 0)
    pick_lane = lax.broadcasted_iota(jnp.int32, (2 * seqs + pad, lanes), 1) % rows
    pick = (pick_lane // tile) * seqs + pick_lane % seqs == pick_row
    bias[...] = lax.dot_general(
        masks, jnp.where(pick, 1.0, 0.0).astype(jnp.bfloat16), (((0,), (0,)), ((), ())),
        preferred_element_type=jnp.float32,
    )

    def fold(x, op):
        return op(x.reshape(x.shape[0] // 8, 8, x.shape[1]), axis=0)

    def score(order, part, top):
        for b in range(part * cut, (part + 1) * cut, STEP):
            got = jnp.dot(
                kbuf[order, b : b + STEP, :], qt[order], preferred_element_type=jnp.float32
            ) + bias[b : b + STEP, :]
            sbuf[order, b : b + STEP, :] = got
            high = fold(got, jnp.max)
            top = high if top is None else jnp.maximum(top, high)
        return top

    def weigh(order, top):
        m = jnp.max(top, axis=0, keepdims=True)
        total = None
        for b in range(0, slots, STEP):
            w = jnp.exp2((sbuf[order, b : b + STEP, :] - m) * SHIFT)
            pbuf[order, :, b : b + STEP] = jnp.transpose(w.astype(jnp.bfloat16))
            part = fold(w, jnp.sum)
            total = part if total is None else total + part
        return jnp.concatenate([m, jnp.sum(total, axis=0, keepdims=True)], axis=0)

    def gather(order, j):
        return jnp.concatenate(
            [
                jnp.dot(
                    pbuf[order, (j * heads_each + e) * rows : (j * heads_each + e + 1) * rows, :],
                    vbuf[order, :, j * width + e * HD : j * width + (e + 1) * HD], preferred_element_type=jnp.float32,
                )
                for e in range(heads_each)
            ],
            axis=0,
        )

    def drain(ref, sem):
        pltpu.make_async_copy(ref, ref, sem).wait()

    rest_sent, ml_sent, first_sent = (isem.at[i] for i in range(3))

    def remote(src, dst, ss, rs, device):
        return pltpu.make_async_remote_copy(
            src_ref=src, dst_ref=dst, send_sem=ss, recv_sem=rs, device_id={"seq": device}, device_id_type=MESH
        )

    def ml_to_partner():
        return remote(half_ml, peer_ml, ml_sent, peer_sem.at[0], partner)

    def num_to_partner(j):
        return remote(half_num.at[j], peer_num.at[j], rest_sent, peer_sem.at[1], partner)

    targets = [0, 1, middle * 2, middle * 2 + 1]
    late = plane // (planes - 1)

    def ml_to_root(i):
        return remote(chip_ml.at[chip], chip_ml.at[chip], ml_sent, ml_sem, targets[i] * 2 + core)

    def num_to_root(j, i):
        sent = rest_sent if i else first_sent
        return remote(chip_num.at[j, chip], chip_num.at[j, chip], sent, num_sem.at[late * (1 + j)], targets[i] * 2 + core)

    def part_of(owner, j):
        return out.at[:, pl.ds(pl.multiple_of(owner * (CHUNKS * span) + j * span, span), span), :]

    def elsewhere(i, act):
        @pl.when(chip != targets[i])
        def _():
            act()

    k_copy(0).wait()
    top = score(0, 0, None)
    k_copy(1).wait()
    top = score(0, 1, top)
    k_copy(2).wait()
    half_ml[...] = weigh(0, top)
    own_top = score(1, 0, None)
    @pl.when(first)
    def _():
        pl.semaphore_wait(barrier, 4)

    @pl.when(central)
    def _():
        pl.semaphore_wait(barrier, 5 + 4 * len(guests))

    @pl.when(guest)
    def _():
        pl.semaphore_wait(barrier, 5)

    ml_to_partner().start()
    v_copy(0).wait()
    for j in range(CHUNKS):
        half_num[j] = gather(0, j).astype(jnp.bfloat16)
    for j in range(CHUNKS):
        num_to_partner(j).start()
    k_copy(3).wait()
    own_top = score(1, 1, own_top)
    ml = weigh(1, own_top)
    drain(peer_ml, peer_sem.at[0])
    other = peer_ml[...]
    top = jnp.maximum(ml[0:1], other[0:1])
    mine = jnp.exp2((ml[0:1] - top) * SHIFT)
    theirs = jnp.exp2((other[0:1] - top) * SHIFT)
    chip_ml[chip] = jnp.concatenate([top, mine * ml[1:2] + theirs * other[1:2]], axis=0)
    columns = jnp.transpose(jnp.concatenate([mine, theirs, jnp.zeros((6, lanes), jnp.float32)], axis=0))
    for i in range(len(targets)):
        elsewhere(i, lambda: ml_to_root(i).start())
    v_copy(1).wait()
    numers = [gather(1, j) for j in range(CHUNKS)]
    drain(peer_num, peer_sem.at[1])
    for j in range(CHUNKS):
        some = slice(j * block, (j + 1) * block)
        total = numers[j] * columns[some, 0:1] + peer_num[j].astype(jnp.float32) * columns[some, 1:2]
        chip_num[j, chip] = total.astype(jnp.bfloat16)
        elsewhere(0, lambda: num_to_root(j, 0).start())
    @pl.when(core == 1)
    def _():
        elsewhere(0, lambda: drain(chip_num.at[0, :CHUNKS], first_sent))

    for j in range(CHUNKS):
        elsewhere(2 + j, lambda: num_to_root(j, 2 + j).start())
    @pl.when(core == 0)
    def _():
        elsewhere(0, lambda: drain(chip_num.at[0, :CHUNKS], first_sent))

    for j in range(CHUNKS):
        elsewhere(1, lambda: num_to_root(j, 1).start())

    def share(j):
        fans = [partner, across, across + 1] + [p * 4 + d for p in guests for d in range(4)]
        return [remote(part_of(core, j), part_of(core, j), rest_sent, fin, device) for device in fans]

    def add_up(j, columns, some, numer):
        for i in some:
            term = chip_num[j, i].astype(jnp.float32) * columns[j * block : (j + 1) * block, i : i + 1]
            numer = term if numer is None else numer + term
        return numer

    def gather_early(j, columns):
        return add_up(j, columns, range(chips - 2), None)

    def collect(j, columns, numer):
        drain(chip_num.at[j, :2], num_sem.at[1 + j])
        attended = add_up(j, columns, range(chips - 2, chips), numer).astype(jnp.bfloat16)
        for e in range(heads_each):
            for t in range(2):
                base = pl.multiple_of(core * (CHUNKS * span) + j * span + e * tile, tile)
                out[t, pl.ds(base, tile), :] = attended[e * rows + t * tile : e * rows + (t + 1) * tile]

    def factors_of_chips():
        drain(chip_ml.at[: chips - 1], ml_sem)
        maxima = [chip_ml[i][0:1] for i in range(chips)]
        top = functools.reduce(jnp.maximum, maxima)
        factors = [jnp.exp2((m - top) * SHIFT) for m in maxima]
        denom = sum(f * chip_ml[i][1:2] for i, f in enumerate(factors))
        factors = [f / denom for f in factors]
        pad = -chips % 8
        if pad:
            factors = factors + [jnp.zeros((pad, lanes), jnp.float32)]
        return jnp.transpose(jnp.concatenate(factors, axis=0))

    @pl.when(first)
    def _():
        columns = factors_of_chips()
        drain(chip_num.at[:, : chips - 3], num_sem.at[0])
        early = [gather_early(j, columns) for j in range(CHUNKS)]
        for j in range(CHUNKS):
            collect(j, columns, early[j])
            remote(part_of(core, j), part_of(core, j), rest_sent, fin, partner).start()

    for j in range(CHUNKS):
        @pl.when(central & (y == j))
        def _():
            columns = factors_of_chips()
            drain(chip_num.at[j, : chips - 3], num_sem.at[0])
            collect(j, columns, gather_early(j, columns))
            for copy in share(j):
                copy.start()

    def sent(units, sem):
        drain(kbuf.at[0, : units * block * HD // wide], sem)

    for who, at_roots, others in (
        (guest, 4, 6), (central, 3, 8 + 4 * len(guests)), (chip == 0, 3, 6 + CHUNKS), (chip == 1, 3, 4 + CHUNKS),
    ):
        @pl.when(who)
        def _():
            drain(chip_ml.at[: 1 + at_roots], ml_sent)
            sent(others, rest_sent)

    @pl.when(first)
    def _():
        drain(out.at[:, : CHUNKS * span], fin)

    @pl.when(central)
    def _():
        drain(out.at[:, : 3 * span], fin)

    @pl.when(guest)
    def _():
        drain(out, fin)


def per_device(n, queries, cache_k, cache_v, context_len, slot_seq, slot_pos):
    slots = cache_k.shape[0]
    seqs = queries.shape[1]
    heads = queries.shape[2] // HD
    rows = 2 * seqs * heads // KVH
    heads_half = KVH // 2
    lanes = heads_half * rows
    block = lanes // CHUNKS
    chips = n // 2
    vmem = pl.BlockSpec(memory_space=pltpu.VMEM)
    dma = pltpu.SemaphoreType.DMA
    anywhere = pl.BlockSpec(memory_space=pltpu.HBM)
    attended = pl.pallas_call(
        functools.partial(kernel, n),
        out_shape=jax.ShapeDtypeStruct((2, heads * seqs, HD), jnp.bfloat16),
        in_specs=[anywhere] * 6,
        out_specs=vmem,
        scratch_shapes=[
            pltpu.SMEM((seqs,), jnp.int32),
            pltpu.VMEM(queries.shape, jnp.bfloat16),
            pltpu.VMEM((2, 1, slots), jnp.int32),
            pltpu.VMEM((2, slots, heads_half * HD), jnp.bfloat16),
            pltpu.VMEM((2, slots, heads_half * HD), jnp.bfloat16),
            pltpu.VMEM((KVH * rows, HD), jnp.float32),
            pltpu.VMEM((2, heads_half * HD, lanes), jnp.bfloat16),
            pltpu.VMEM((slots, lanes), jnp.float32),
            pltpu.VMEM((2, slots, lanes), jnp.float32),
            pltpu.VMEM((2, lanes, slots), jnp.bfloat16),
            pltpu.VMEM((CHUNKS, block, HD), jnp.bfloat16),
            pltpu.VMEM((2, lanes), jnp.float32),
            pltpu.VMEM((CHUNKS, block, HD), jnp.bfloat16),
            pltpu.VMEM((2, lanes), jnp.float32),
            pltpu.VMEM((CHUNKS, chips, block, HD), jnp.bfloat16),
            pltpu.VMEM((chips, 2, lanes), jnp.float32),
            dma((3,)), dma((2 * CHUNKS,)), dma((2,)), dma((2,)), dma(()), dma((1 + CHUNKS,)), dma(()),
        ],
        compiler_params=pltpu.CompilerParams(collective_id=0, has_side_effects=True, vmem_limit_bytes=LIMIT),
    )(*[
        pltpu.with_memory_space_constraint(x, pltpu.HBM)
        for x in (context_len, queries, cache_k, cache_v, slot_seq.reshape(1, slots), slot_pos.reshape(1, slots))
    ])
    steps = queries.shape[0]
    return attended.reshape(steps, heads, seqs, HD).transpose(0, 2, 1, 3).reshape(queries.shape)


def solution(mesh):
    return jax.shard_map(
        functools.partial(per_device, mesh.shape["seq"]),
        mesh=mesh,
        in_specs=(
            P(None, "parts", None),
            P(("parts", "seq"), None),
            P(("parts", "seq"), None),
            P("parts"),
            P(("parts", "seq")),
            P(("parts", "seq")),
        ),
        out_specs=P(None, "parts", None),
        check_vma=False,
    )
```

```python
import functools

import jax
import jax.numpy as jnp
from jax import lax
from jax.experimental import pallas as pl
from jax.experimental.pallas import tpu as pltpu
from jax.sharding import PartitionSpec as P

KVH = 8
HD = 128
CHUNKS = 2
STEP = 256
LIMIT = 24 << 20
SHIFT = HD ** (-0.5) * 1.4426950408889634
HIDDEN = -1e30
MESH = pl.DeviceIdType.MESH


def kernel(
    n, ctx_hbm, q_hbm, k_hbm, v_hbm, seq_hbm, pos_hbm, out,
    ctx, q_ref, slot_ref, kbuf, vbuf, qf, qt, bias, sbuf, pbuf,
    half_num, half_ml, peer_num, peer_ml, chip_num, chip_ml,
    isem, ksem, vsem, peer_sem, ml_sem, num_sem, fin,
):
    me = lax.axis_index("seq")
    chips = n // 2
    planes = chips // 2
    core = me % 2
    chip = me // 2
    y = chip % 2
    plane = chip // 2
    middle = planes // 2
    first, central = plane == 0, plane == middle
    guests = [p for p in range(planes) if p not in (0, middle)]
    guest = jnp.logical_not(first | central)
    partner = chip * 2 + (1 - core)
    across = (plane * 2 + (1 - y)) * 2
    halves = (1 - core, core)
    slots = k_hbm.shape[0]
    heads_half = KVH // 2
    heads_each = heads_half // CHUNKS
    wide = heads_half * HD
    width = heads_each * HD
    group = q_ref.shape[2] // HD // KVH
    seqs = q_ref.shape[1]
    rows = 2 * seqs * group
    lanes = heads_half * rows
    block = heads_each * rows
    tile = group * seqs
    span = heads_each * tile
    cut = slots // CHUNKS

    barrier = pltpu.get_barrier_semaphore()

    def greet(device):
        pl.semaphore_signal(barrier, inc=1, device_id={"seq": device}, device_id_type=MESH)

    seq_ref, pos_ref = slot_ref.at[0], slot_ref.at[1]
    inputs = []
    for i, src, dst in ((0, q_hbm, q_ref), (1, seq_hbm, seq_ref), (1, pos_hbm, pos_ref), (2, ctx_hbm, ctx)):
        copy = pltpu.make_async_copy(src, dst, isem.at[i])
        copy.start()
        inputs.append(copy)

    def first_column(order):
        half = core * order + (1 - core) * (1 - order)
        return half * wide

    def k_copy(i):
        order, part = i // CHUNKS, i % CHUNKS
        some = pl.ds(pl.multiple_of(part * cut, cut), cut)
        columns = pl.ds(pl.multiple_of(first_column(order), wide), wide)
        return pltpu.make_async_copy(k_hbm.at[some, columns], kbuf.at[order, some], ksem.at[i])

    def v_copy(order):
        columns = pl.ds(pl.multiple_of(first_column(order), wide), wide)
        return pltpu.make_async_copy(v_hbm.at[:, columns], vbuf.at[order], vsem.at[order])

    def load_k(i, carry):
        k_copy(i).start()
        return carry

    def load_v(order, carry):
        v_copy(order).start()

        @pl.when(order == 0)
        def _():
            k_copy(2 * CHUNKS - 1).start()

        return carry

    lax.fori_loop(0, 2 * CHUNKS - 1, load_k, 0)
    lax.fori_loop(0, 2, load_v, 0)

    greet(partner)

    @pl.when(first | central)
    def _():
        for k in range(1, chips):
            greet((chip + k) % chips * 2 + core)

    @pl.when(central)
    def _():
        greet(across + (1 - core))

    @pl.when(guest)
    def _():
        for d in range(4):
            greet(middle * 4 + d)

    inputs[0].wait()
    pltpu.make_async_copy(slot_ref, slot_ref, isem.at[1]).wait()
    inputs[3].wait()

    for t in range(2):
        for head in range(KVH * group):
            g, h = head // group, head % group
            base = g * rows + t * group * seqs + h * seqs
            qf[base : base + seqs, :] = q_ref[t, :, head * HD : (head + 1) * HD].astype(jnp.float32)

    column = lax.broadcasted_iota(jnp.int32, (HD, lanes), 1)
    for order in range(2):
        turned = jnp.transpose(qf[pl.ds(pl.multiple_of(halves[order] * lanes, lanes), lanes), :])
        for e in range(heads_half):
            qt[order, e * HD : (e + 1) * HD, :] = jnp.where(column // rows == e, turned, 0.0).astype(jnp.bfloat16)

    masks = []
    for t in range(2):
        for sq in range(seqs):
            allowed = (seq_ref[...] == sq) & (pos_ref[...] <= ctx[sq] - 2 + t)
            masks.append(jnp.where(allowed, 0.0, HIDDEN))
    pad = -len(masks) % 16
    masks = jnp.concatenate(masks + [jnp.zeros((pad, slots), jnp.float32)], axis=0).astype(jnp.bfloat16)
    pick_row = lax.broadcasted_iota(jnp.int32, (2 * seqs + pad, lanes), 0)
    pick_lane = lax.broadcasted_iota(jnp.int32, (2 * seqs + pad, lanes), 1) % rows
    pick = (pick_lane // tile) * seqs + pick_lane % seqs == pick_row
    bias[...] = lax.dot_general(
        masks, jnp.where(pick, 1.0, 0.0).astype(jnp.bfloat16), (((0,), (0,)), ((), ())),
        preferred_element_type=jnp.float32,
    )

    def fold(x, op):
        return op(x.reshape(x.shape[0] // 8, 8, x.shape[1]), axis=0)

    def score(order, part, top):
        for b in range(part * cut, (part + 1) * cut, STEP):
            got = jnp.dot(
                kbuf[order, b : b + STEP, :], qt[order], preferred_element_type=jnp.float32
            ) + bias[b : b + STEP, :]
            sbuf[order, b : b + STEP, :] = got
            high = fold(got, jnp.max)
            top = high if top is None else jnp.maximum(top, high)
        return top

    def weigh(order, top):
        m = jnp.max(top, axis=0, keepdims=True)
        total = None
        for b in range(0, slots, STEP):
            w = jnp.exp2((sbuf[order, b : b + STEP, :] - m) * SHIFT)
            pbuf[order, :, b : b + STEP] = jnp.transpose(w.astype(jnp.bfloat16))
            part = fold(w, jnp.sum)
            total = part if total is None else total + part
        return jnp.concatenate([m, jnp.sum(total, axis=0, keepdims=True)], axis=0)

    def gather(order, j):
        return jnp.concatenate(
            [
                jnp.dot(
                    pbuf[order, (j * heads_each + e) * rows : (j * heads_each + e + 1) * rows, :],
                    vbuf[order, :, j * width + e * HD : j * width + (e + 1) * HD], preferred_element_type=jnp.float32,
                )
                for e in range(heads_each)
            ],
            axis=0,
        )

    def drain(ref, sem):
        pltpu.make_async_copy(ref, ref, sem).wait()

    rest_sent, ml_sent, first_sent = (isem.at[i] for i in range(3))

    def remote(src, dst, ss, rs, device):
        return pltpu.make_async_remote_copy(
            src_ref=src, dst_ref=dst, send_sem=ss, recv_sem=rs, device_id={"seq": device}, device_id_type=MESH
        )

    def ml_to_partner():
        return remote(half_ml, peer_ml, ml_sent, peer_sem.at[0], partner)

    def num_to_partner(j):
        return remote(half_num.at[j], peer_num.at[j], rest_sent, peer_sem.at[1], partner)

    targets = [0, 1, middle * 2, middle * 2 + 1]
    late = plane // (planes - 1)

    def ml_to_root(i):
        return remote(chip_ml.at[chip], chip_ml.at[chip], ml_sent, ml_sem, targets[i] * 2 + core)

    def num_to_root(j, i):
        sent = rest_sent if i else first_sent
        return remote(chip_num.at[j, chip], chip_num.at[j, chip], sent, num_sem.at[late * (1 + j)], targets[i] * 2 + core)

    def part_of(owner, j):
        return out.at[:, pl.ds(pl.multiple_of(owner * (CHUNKS * span) + j * span, span), span), :]

    def elsewhere(i, act):
        @pl.when(chip != targets[i])
        def _():
            act()

    k_copy(0).wait()
    top = score(0, 0, None)
    k_copy(1).wait()
    k_copy(2).wait()
    top = score(0, 1, top)
    own_top = score(1, 0, None)
    half_ml[...] = weigh(0, top)
    @pl.when(first)
    def _():
        pl.semaphore_wait(barrier, 4)

    @pl.when(central)
    def _():
        pl.semaphore_wait(barrier, 5 + 4 * len(guests))

    @pl.when(guest)
    def _():
        pl.semaphore_wait(barrier, 5)

    ml_to_partner().start()
    v_copy(0).wait()
    for j in range(CHUNKS):
        half_num[j] = gather(0, j).astype(jnp.bfloat16)
    for j in range(CHUNKS):
        num_to_partner(j).start()
    k_copy(3).wait()
    own_top = score(1, 1, own_top)
    ml = weigh(1, own_top)
    drain(peer_ml, peer_sem.at[0])
    other = peer_ml[...]
    top = jnp.maximum(ml[0:1], other[0:1])
    mine = jnp.exp2((ml[0:1] - top) * SHIFT)
    theirs = jnp.exp2((other[0:1] - top) * SHIFT)
    chip_ml[chip] = jnp.concatenate([top, mine * ml[1:2] + theirs * other[1:2]], axis=0)
    columns = jnp.transpose(jnp.concatenate([mine, theirs, jnp.zeros((6, lanes), jnp.float32)], axis=0))
    for i in range(len(targets)):
        elsewhere(i, lambda: ml_to_root(i).start())
    v_copy(1).wait()
    numers = [gather(1, j) for j in range(CHUNKS)]
    drain(peer_num, peer_sem.at[1])
    for j in range(CHUNKS):
        some = slice(j * block, (j + 1) * block)
        total = numers[j] * columns[some, 0:1] + peer_num[j].astype(jnp.float32) * columns[some, 1:2]
        chip_num[j, chip] = total.astype(jnp.bfloat16)
        elsewhere(0, lambda: num_to_root(j, 0).start())
    @pl.when(core == 1)
    def _():
        elsewhere(0, lambda: drain(chip_num.at[0, :CHUNKS], first_sent))

    for j in range(CHUNKS):
        elsewhere(2 + j, lambda: num_to_root(j, 2 + j).start())
    @pl.when(core == 0)
    def _():
        elsewhere(0, lambda: drain(chip_num.at[0, :CHUNKS], first_sent))

    for j in range(CHUNKS):
        elsewhere(1, lambda: num_to_root(j, 1).start())

    def share(j):
        fans = [partner, across, across + 1] + [p * 4 + d for p in guests for d in range(4)]
        return [remote(part_of(core, j), part_of(core, j), rest_sent, fin, device) for device in fans]

    def add_up(j, columns, some, numer):
        for i in some:
            term = chip_num[j, i].astype(jnp.float32) * columns[j * block : (j + 1) * block, i : i + 1]
            numer = term if numer is None else numer + term
        return numer

    def gather_early(j, columns):
        return add_up(j, columns, range(chips - 2), None)

    def collect(j, columns, numer):
        drain(chip_num.at[j, :2], num_sem.at[1 + j])
        attended = add_up(j, columns, range(chips - 2, chips), numer).astype(jnp.bfloat16)
        for e in range(heads_each):
            for t in range(2):
                base = pl.multiple_of(core * (CHUNKS * span) + j * span + e * tile, tile)
                out[t, pl.ds(base, tile), :] = attended[e * rows + t * tile : e * rows + (t + 1) * tile]

    def factors_of_chips():
        drain(chip_ml.at[: chips - 1], ml_sem)
        maxima = [chip_ml[i][0:1] for i in range(chips)]
        top = functools.reduce(jnp.maximum, maxima)
        factors = [jnp.exp2((m - top) * SHIFT) for m in maxima]
        denom = sum(f * chip_ml[i][1:2] for i, f in enumerate(factors))
        factors = [f / denom for f in factors]
        pad = -chips % 8
        if pad:
            factors = factors + [jnp.zeros((pad, lanes), jnp.float32)]
        return jnp.transpose(jnp.concatenate(factors, axis=0))

    @pl.when(first)
    def _():
        columns = factors_of_chips()
        drain(chip_num.at[:, : chips - 3], num_sem.at[0])
        early = [gather_early(j, columns) for j in range(CHUNKS)]
        for j in range(CHUNKS):
            collect(j, columns, early[j])
            remote(part_of(core, j), part_of(core, j), rest_sent, fin, partner).start()

    for j in range(CHUNKS):
        @pl.when(central & (y == j))
        def _():
            columns = factors_of_chips()
            drain(chip_num.at[j, : chips - 3], num_sem.at[0])
            collect(j, columns, gather_early(j, columns))
            for copy in share(j):
                copy.start()

    def sent(units, sem):
        drain(kbuf.at[0, : units * block * HD // wide], sem)

    for who, at_roots, others in (
        (guest, 4, 6), (central, 3, 8 + 4 * len(guests)), (chip == 0, 3, 6 + CHUNKS), (chip == 1, 3, 4 + CHUNKS),
    ):
        @pl.when(who)
        def _():
            drain(chip_ml.at[: 1 + at_roots], ml_sent)
            sent(others, rest_sent)

    @pl.when(first)
    def _():
        drain(out.at[:, : CHUNKS * span], fin)

    @pl.when(central)
    def _():
        drain(out.at[:, : 3 * span], fin)

    @pl.when(guest)
    def _():
        drain(out, fin)


def per_device(n, queries, cache_k, cache_v, context_len, slot_seq, slot_pos):
    slots = cache_k.shape[0]
    seqs = queries.shape[1]
    heads = queries.shape[2] // HD
    rows = 2 * seqs * heads // KVH
    heads_half = KVH // 2
    lanes = heads_half * rows
    block = lanes // CHUNKS
    chips = n // 2
    vmem = pl.BlockSpec(memory_space=pltpu.VMEM)
    dma = pltpu.SemaphoreType.DMA
    anywhere = pl.BlockSpec(memory_space=pltpu.HBM)
    attended = pl.pallas_call(
        functools.partial(kernel, n),
        out_shape=jax.ShapeDtypeStruct((2, heads * seqs, HD), jnp.bfloat16),
        in_specs=[anywhere] * 6,
        out_specs=vmem,
        scratch_shapes=[
            pltpu.SMEM((seqs,), jnp.int32),
            pltpu.VMEM(queries.shape, jnp.bfloat16),
            pltpu.VMEM((2, 1, slots), jnp.int32),
            pltpu.VMEM((2, slots, heads_half * HD), jnp.bfloat16),
            pltpu.VMEM((2, slots, heads_half * HD), jnp.bfloat16),
            pltpu.VMEM((KVH * rows, HD), jnp.float32),
            pltpu.VMEM((2, heads_half * HD, lanes), jnp.bfloat16),
            pltpu.VMEM((slots, lanes), jnp.float32),
            pltpu.VMEM((2, slots, lanes), jnp.float32),
            pltpu.VMEM((2, lanes, slots), jnp.bfloat16),
            pltpu.VMEM((CHUNKS, block, HD), jnp.bfloat16),
            pltpu.VMEM((2, lanes), jnp.float32),
            pltpu.VMEM((CHUNKS, block, HD), jnp.bfloat16),
            pltpu.VMEM((2, lanes), jnp.float32),
            pltpu.VMEM((CHUNKS, chips, block, HD), jnp.bfloat16),
            pltpu.VMEM((chips, 2, lanes), jnp.float32),
            dma((3,)), dma((2 * CHUNKS,)), dma((2,)), dma((2,)), dma(()), dma((1 + CHUNKS,)), dma(()),
        ],
        compiler_params=pltpu.CompilerParams(collective_id=0, has_side_effects=True, vmem_limit_bytes=LIMIT),
    )(*[
        pltpu.with_memory_space_constraint(x, pltpu.HBM)
        for x in (context_len, queries, cache_k, cache_v, slot_seq.reshape(1, slots), slot_pos.reshape(1, slots))
    ])
    steps = queries.shape[0]
    return attended.reshape(steps, heads, seqs, HD).transpose(0, 2, 1, 3).reshape(queries.shape)


def solution(mesh):
    return jax.shard_map(
        functools.partial(per_device, mesh.shape["seq"]),
        mesh=mesh,
        in_specs=(
            P(None, "parts", None),
            P(("parts", "seq"), None),
            P(("parts", "seq"), None),
            P("parts"),
            P(("parts", "seq")),
            P(("parts", "seq")),
        ),
        out_specs=P(None, "parts", None),
        check_vma=False,
    )
```
